256 devices in a mesh: gx: 8 (over z), gy: 32 (over x, y, core).
Axes of the slice: x: 4, y: 4, z: 8, core: 2. Of those that a mesh axis runs over, the one named last changes fastest.
Arguments:
- orbitals: float32 [2, 256, 512, 256], P(None, 'gx', 'gy'), may hold values from -6 to 6
- potential: float32 [256, 512, 256], P('gx', 'gy'), may hold values from -4 to 4
- projectors: float32 [8192, 9, 1024], P(('gx', 'gy')), may hold values from -3 to 3
- strengths: float32 [9], replicated, may hold values from 0.5 to 2
- atom_owner: int32 [5120], replicated, may hold values from 0 to 255, as said below
- slot_atom: int32 [8192], P(('gx', 'gy')), may hold values from 0 to 5120, as said below
- slot_offset: int32 [3, 8192], P(None, ('gx', 'gy')), may hold values from 0 to 240, as said below
Outputs:
- first_filter: float32 [2, 256, 512, 256], P(None, 'gx', 'gy')
- second_filter: float32 [2, 256, 512, 256], P(None, 'gx', 'gy')
The draws below stay inside these ranges and needn't reach their ends.
Inputs may be any that keep to these rules, and one draw needn't show every extreme that they name: `atom_owner`: every tile owns 1 to 39 atoms, and some tile owns exactly 39. `slot_atom`: every live slot is linked; the first slots of a tile are live and the rest empty; at most 32 live slots a tile, and some tile has empty slots. `slot_offset`: A patch lies within its tile: the first entry is at most 24, the second at most 8, the third at most 240, which some slot reaches.
All inputs are finite; a program needn't handle non-finite values.
Results may differ from the reference program's by a relative error of at most 0.00012.
Values sent between devices are 32-bit elements; how exact they have to be, the bound alone decides.
No kernel may reach another device: no remote copies, remote signals or barrier semaphores. Data moves between devices by JAX's collectives and lax.ppermute only.
A program may use at most 64 MiB of HBM per device.

```python
import math
import jax
import jax.numpy as jnp
from jax import lax

CX = 32
CY = 16
NZ = 256
ATOM_DEV = 20
KSLOT = 32
ORB = 2
NPROJ = 9
BXY = 8
BZ = 16
BOX = 1024
ATOMS = 5120
SLOTS = 8192
NX = 256
NY = 512
N_GX = 8
N_GY = 32


def owner_table(key):
    base_key = jax.random.fold_in(key, 101)
    device_count = N_GX * N_GY
    pair_count = device_count // 2
    key_moved, key_fullest, key_shuffle = jax.random.split(base_key, 3)
    moved = jax.random.randint(key_moved, (pair_count,), 0, ATOM_DEV)
    fullest = jax.random.randint(key_fullest, (), 0, pair_count)
    moved = jnp.where(jnp.arange(pair_count) == fullest, ATOM_DEV - 1, moved)
    places = jnp.arange(ATOMS, dtype=jnp.int32)
    tile_of = places // ATOM_DEV
    position = places % ATOM_DEV
    moved_back = (tile_of % 2 == 1) & (position < moved[tile_of // 2])
    tile_of = jnp.where(moved_back, tile_of - 1, tile_of)
    shuffle = jax.random.permutation(key_shuffle, ATOMS)
    return tile_of[shuffle].astype(jnp.int32)


def draw_atom_owner(key, part):
    return owner_table(key)


def draw_slot_atom(key, part):
    owner_tile = owner_table(key)
    device_count = N_GX * N_GY
    counts = jnp.sum((owner_tile[None, :] == jnp.arange(device_count)[:, None]).astype(jnp.int32), axis=1)
    starts = jnp.cumsum(counts) - counts
    sorted_atoms = jnp.argsort(owner_tile, stable=True).astype(jnp.int32)
    slot_key = jax.random.fold_in(key, 202)
    key_live, key_dir, key_rank, key_low = jax.random.split(slot_key, 4)
    live_count = jax.random.randint(key_live, (device_count,), KSLOT // 2, KSLOT + 1)
    lowest = jax.random.randint(key_low, (), 0, device_count)
    live_count = jnp.where(jnp.arange(device_count) == lowest, KSLOT // 2, live_count)
    device = jnp.arange(device_count)[:, None]
    slot_pos = jnp.arange(KSLOT)[None, :]
    direction = jax.random.randint(key_dir, (device_count, KSLOT), 0, 9)
    step_x = direction // 3 - 1
    step_y = direction % 3 - 1
    nearby = (device // N_GY + step_x) % N_GX * N_GY + (device % N_GY + step_y) % N_GY
    owner_rank = jax.random.randint(key_rank, (device_count, KSLOT), 0, counts[nearby])
    atoms_hit = sorted_atoms[starts[nearby] + owner_rank]
    atoms_hit = jnp.where(slot_pos < live_count[:, None], atoms_hit, ATOMS)
    return atoms_hit.reshape(-1).astype(jnp.int32)


def draw_slot_offset(key, part):
    total_slots = N_GX * N_GY * KSLOT
    offset_key = jax.random.fold_in(key, 303)
    key_x, key_y, key_z, key_pick = jax.random.split(offset_key, 4)
    corner_x = jax.random.randint(key_x, (total_slots,), 0, CX - BXY + 1)
    corner_y = jax.random.randint(key_y, (total_slots,), 0, CY - BXY + 1)
    corner_z = jax.random.randint(key_z, (total_slots,), 0, NZ - BZ + 1)
    picked = jax.random.randint(key_pick, (), 0, total_slots)
    corner_z = jnp.where(jnp.arange(total_slots) == picked, NZ - BZ, corner_z)
    corner_x = jnp.where(jnp.arange(total_slots) == picked, CX - BXY, corner_x)
    corner_y = jnp.where(jnp.arange(total_slots) == picked, CY - BXY, corner_y)
    return jnp.stack([corner_x, corner_y, corner_z]).astype(jnp.int32)


def block_levels(own_key, shape, cuts, smallest, largest):
    loudness, own = 1.0, jax.random.fold_in(own_key, 6)
    for dim, parts in cuts:
        steps = jnp.exp(jax.random.uniform(jax.random.fold_in(own, dim), (parts,), jnp.float32, smallest / len(cuts), largest / len(cuts)))
        loudness = loudness * jnp.repeat(steps, shape[dim] // parts).reshape([-1 if axis == dim else 1 for axis in range(len(shape))])
    return loudness


def gaussian(own_key, extent, scale, most, pieces=(), held_as=jnp.bfloat16):
    gain = block_levels(own_key, extent, pieces, -0.22, 0.18) if pieces else 1.0
    values = jax.random.normal(own_key, extent, jnp.float32) * scale * gain
    return jnp.minimum(jnp.maximum(values, -most), most).astype(held_as)


def setup_inputs(seed: int = 0) -> dict:
    splits = jax.random.split(jax.random.key(seed), 8)
    orbitals = gaussian(splits[0], (ORB, NX, NY, NZ), 1.0, 6.0, ((1, 8), (2, 32)), jnp.float32)
    potential = jnp.clip(jax.random.uniform(splits[1], (NX, NY, NZ), jnp.float32, -4.0, 4.0) * block_levels(splits[1], (NX, NY, NZ), ((0, 8), (1, 32)), -0.4, 0.0), -4.0, 4.0)
    projectors = gaussian(splits[2], (SLOTS, NPROJ, BOX), 0.5, 3.0, ((0, 256),), jnp.float32)
    strengths = jnp.clip(jnp.exp(jax.random.uniform(splits[3], (NPROJ,), jnp.float32, math.log(0.5), math.log(2.0))), 0.5, 2.0)
    atom_owner = draw_atom_owner(jax.random.fold_in(splits[7], 71), 0)
    slot_atom = draw_slot_atom(jax.random.fold_in(splits[7], 71), 0)
    slot_offset = draw_slot_offset(jax.random.fold_in(splits[7], 71), 0)
    return dict(orbitals=orbitals, potential=potential, projectors=projectors, strengths=strengths, atom_owner=atom_owner, slot_atom=slot_atom, slot_offset=slot_offset)


LAPLACE_COEFFS = (-5369.0 / 1800.0, 12.0 / 7.0, -15.0 / 56.0, 10.0 / 189.0, -1.0 / 112.0, 2.0 / 1925.0, -1.0 / 16632.0)
SPACING = 0.4
CENTER = 45.0
HALF_WIDTH = 48.0


def kinetic(orbital):
    depth = orbital.shape[3]
    padded_z = jnp.pad(orbital, ((0, 0), (0, 0), (0, 0), (6, 6)))
    summed = (3.0 * LAPLACE_COEFFS[0]) * orbital
    for reach in range(1, 7):
        paired = jnp.roll(orbital, reach, 1) + jnp.roll(orbital, -reach, 1)
        paired = paired + jnp.roll(orbital, reach, 2) + jnp.roll(orbital, -reach, 2)
        paired = paired + padded_z[:, :, :, 6 + reach:6 + reach + depth] + padded_z[:, :, :, 6 - reach:6 - reach + depth]
        summed = summed + LAPLACE_COEFFS[reach] * paired
    return (-0.5 / (SPACING * SPACING)) * summed


def patch_index(slot_offset, size_y, size_z):
    slot_count = slot_offset.shape[1]
    device = jnp.arange(slot_count, dtype=jnp.int32) // KSLOT
    corner_x = (device // N_GY) * CX + slot_offset[0]
    corner_y = (device % N_GY) * CY + slot_offset[1]
    cell_ids = jnp.arange(BOX, dtype=jnp.int32)
    step_x = cell_ids // (BXY * BZ)
    step_y = (cell_ids // BZ) % BXY
    step_z = cell_ids % BZ
    pos_x = corner_x[:, None] + step_x[None, :]
    pos_y = corner_y[:, None] + step_y[None, :]
    pos_z = slot_offset[2][:, None] + step_z[None, :]
    return ((pos_x * size_y + pos_y) * size_z + pos_z).astype(jnp.int32)


def linked_slots(atom_owner, slot_atom):
    slot_count = slot_atom.shape[0]
    device = jnp.arange(slot_count, dtype=jnp.int32) // KSLOT
    safe_atom = jnp.minimum(slot_atom, ATOMS - 1)
    owner_tile = atom_owner[safe_atom]
    step_x = (owner_tile // N_GY - device // N_GY + 1) % N_GX - 1
    step_y = (owner_tile % N_GY - device % N_GY + 1) % N_GY - 1
    return (slot_atom < ATOMS) & (step_x <= 1) & (step_y <= 1)


def nonlocal_term(orbital, projectors, strengths, slot_atom, linked, flat_index):
    flat_field = orbital.reshape(orbital.shape[0], -1)
    patches = flat_field[:, flat_index]
    partial_value = jnp.einsum("spc,osc->spo", projectors, patches, precision=lax.Precision.HIGHEST)
    target = jnp.where(linked, slot_atom, ATOMS).astype(jnp.int32)
    atom_table = jax.ops.segment_sum(partial_value * linked.astype(jnp.float32)[:, None, None], target, num_segments=ATOMS + 1)
    coefficient = atom_table[target] * linked.astype(jnp.float32)[:, None, None] * strengths[None, :, None]
    added = jnp.einsum("spc,spo->osc", projectors, coefficient, precision=lax.Precision.HIGHEST)
    result = jnp.zeros_like(flat_field).at[:, flat_index].add(added)
    return result.reshape(orbital.shape)


def reference(orbitals, potential, projectors, strengths, atom_owner, slot_atom, slot_offset):
    flat_index = patch_index(slot_offset, orbitals.shape[2], orbitals.shape[3])
    linked = linked_slots(atom_owner, slot_atom)

    def hamiltonian(orbital):
        return kinetic(orbital) + potential[None] * orbital + nonlocal_term(orbital, projectors, strengths, slot_atom, linked, flat_index)

    first_filter = (hamiltonian(orbitals) - CENTER * orbitals) / HALF_WIDTH
    second_filter = 2.0 * (hamiltonian(first_filter) - CENTER * first_filter) / HALF_WIDTH - orbitals
    return (first_filter, second_filter)
```

```python
import jax
import jax.numpy as jnp
from jax import lax
from jax.experimental import pallas as pl
from jax.experimental.pallas import tpu as pltpu
from jax.sharding import PartitionSpec as P

LAPLACE_COEFFS = (
    -5369.0 / 1800.0,
    12.0 / 7.0,
    -15.0 / 56.0,
    10.0 / 189.0,
    -1.0 / 112.0,
    2.0 / 1925.0,
    -1.0 / 16632.0,
)
SPACING = 0.4
CENTER = 45.0
HALF_WIDTH = 48.0
KINETIC = -0.5 / (SPACING * SPACING)
REACH = 6

ORB = 2
NPROJ = 9
LANES = 128
CX, CY, NZ = 32, 16, 256
SLOTS = 32
ATOMS = 5120
BLOCK = 40
WIDTH = 24
Y_ROWS = ORB * CX * 2 * 8
X_ROWS = ORB * REACH * 2 * CY

VMEM = pl.BlockSpec(memory_space=pltpu.VMEM)
SMEM = pl.BlockSpec(memory_space=pltpu.SMEM)
F32 = jnp.float32


def iota(shape, axis):
    return lax.broadcasted_iota(jnp.int32, shape, axis)


def swap_groups(x):
    row = iota((1, 8, LANES), 1)
    group = iota((1, 8, LANES), 2) // 16
    for d in (4, 2, 1):
        row_bit, group_bit = ((row & d) != 0, (group & d) != 0)
        later = pltpu.roll(pltpu.roll(x, 8 - d, 1), 16 * d, 2)
        if d == 4:
            other = later
        else:
            earlier = pltpu.roll(pltpu.roll(x, d, 1), LANES - 16 * d, 2)
            other = jnp.where(group_bit, later, earlier)
        x = jnp.where(row_bit == group_bit, x, other)
    return x


def corner(offset_ref, slot):
    z = offset_ref[2, slot]
    return offset_ref[0, slot], offset_ref[1, slot], z // LANES, z % LANES


def project(work, proj_ref, offset_ref, atom_ref, part):
    lane = iota((1, 8, LANES), 2)
    group_of_lane = lane // 16
    flat_lane = iota((8, LANES), 1)

    def group_step(g, carry):
        patches = [jnp.zeros((8, 8, LANES), F32) for _ in range(ORB)]
        for i in range(8):
            x, y, half, z = corner(offset_ref, g * 8 + i)
            shift = (16 * i + LANES - z) % LANES
            for o in range(ORB):
                near = work[o, pl.ds(x, 8), half, pl.ds(y, 8), :]
                far = work[o, pl.ds(x, 8), 1, pl.ds(y, 8), :]
                window = pltpu.roll(jnp.where(lane >= z, near, far), shift, 2)
                patches[o] = jnp.where(group_of_lane == i, window, patches[o])
        patches = [swap_groups(patch) for patch in patches]
        tile = jnp.zeros((8, LANES), F32)
        rows = pl.ds(pl.multiple_of(g * 8, 8), 8)
        for p in range(NPROJ):
            values = [proj_ref[p, rows, LANES * a : LANES * (a + 1)] for a in range(8)]
            for o in range(ORB):
                total = values[0] * patches[o][0]
                for a in range(1, 8):
                    total = total + values[a] * patches[o][a]
                summed = jnp.sum(total, axis=1, keepdims=True)
                tile = jnp.where(flat_lane == 2 * p + o, summed, tile)
        part[rows, :] = tile
        return carry

    lax.fori_loop(0, SLOTS // 8, group_step, 0)
    atoms = jnp.full((8, LANES), -2.0, F32)
    first = iota((8, LANES), 0) == 0
    for s in range(SLOTS):
        atoms = jnp.where(first & (flat_lane == s), atom_ref[s].astype(F32), atoms)
    part[SLOTS:BLOCK, :] = atoms


def pack(work, part, y_up, y_down, x_up, x_down):
    for o in range(ORB):
        rows = slice(o * CX * 16, (o + 1) * CX * 16)
        y_up[rows, :] = work[o, :, :, 8:16, :].reshape(CX * 16, LANES)
        y_down[rows, :] = work[o, :, :, 0:8, :].reshape(CX * 16, LANES)
        rows = slice(o * REACH * 32, (o + 1) * REACH * 32)
        x_up[rows, :] = work[o, CX - REACH : CX].reshape(REACH * 32, LANES)
        x_down[rows, :] = work[o, 0:REACH].reshape(REACH * 32, LANES)
    y_up[Y_ROWS:, :] = part[...]
    y_down[Y_ROWS:, :] = part[...]


def first_kernel(v, proj_ref, offset_ref, atom_ref, y_up, y_down, x_up, x_down, part, work):
    for half in range(2):
        work[:, :, half] = v[:, :, :, LANES * half : LANES * (half + 1)]
    project(work, proj_ref, offset_ref, atom_ref, part)
    pack(work, part, y_up, y_down, x_up, x_down)


def local_kernel(scale, subtract, *refs):
    if subtract:
        v, potential, before, after, orbital, out, pad, along_z = refs
    else:
        v, potential, before, after, out, pad, along_z = refs
    weights = [scale * KINETIC / HALF_WIDTH * w for w in LAPLACE_COEFFS]

    gap = jnp.abs(iota((NZ, NZ), 0) - iota((NZ, NZ), 1))
    band = jnp.zeros((NZ, NZ), F32)
    for r in range(1, REACH + 1):
        band = jnp.where(gap == r, weights[r], band)
    along_z[...] = jnp.dot(
        v[...].reshape(ORB * CX * CY, NZ),
        band,
        precision=lax.Precision.HIGHEST,
        preferred_element_type=F32,
    )

    for o in range(ORB):
        for x in range(REACH):
            pad[o, x, :, 8:24, :] = jnp.zeros((2, CY, LANES), F32)
            pad[o, x + REACH + CX, :, 8:24, :] = jnp.zeros((2, CY, LANES), F32)
        rows = slice(o * CX * 16, (o + 1) * CX * 16)
        pad[o, REACH : REACH + CX, :, 0:8, :] = before[rows, :].reshape(CX, 2, 8, LANES)
        pad[o, REACH : REACH + CX, :, 24:32, :] = after[rows, :].reshape(CX, 2, 8, LANES)
        for half in range(2):
            pad[o, REACH : REACH + CX, half, 8:24, :] = v[
                o, :, :, LANES * half : LANES * (half + 1)
            ]

    def step(n, carry):
        o, x = (n // CX, n % CX)
        for half in range(2):
            lanes = slice(LANES * half, LANES * (half + 1))
            for t in range(2):
                rows = slice(8 + 8 * t, 16 + 8 * t)
                here = pad[o, x + REACH, half, rows, :]
                factor = potential[x, 8 * t : 8 * t + 8, lanes] * (scale / HALF_WIDTH) + (
                    3.0 * weights[0] - scale * CENTER / HALF_WIDTH
                )
                total = factor * here
                depth = pl.ds(pl.multiple_of(n * CY + 8 * t, 8), 8)
                total = total + along_z[depth, lanes]
                for r in range(1, REACH + 1):
                    paired = (
                        pad[o, x + REACH + r, half, rows, :] + pad[o, x + REACH - r, half, rows, :]
                    )
                    paired = paired + (
                        pad[o, x + REACH, half, 8 + 8 * t + r : 16 + 8 * t + r, :]
                        + pad[o, x + REACH, half, 8 + 8 * t - r : 16 + 8 * t - r, :]
                    )
                    total = total + weights[r] * paired
                if subtract:
                    total = total - orbital[o, x, 8 * t : 8 * t + 8, lanes]
                out[o, x, half, 8 * t : 8 * t + 8, :] = total
        return carry

    lax.fori_loop(0, ORB * CX, step, 0)


def coefficients(tiles, atom_ref):
    row = iota((SLOTS, LANES), 0)
    own = jnp.full((SLOTS, LANES), -1.0, F32)
    for s in range(SLOTS):
        atom = jnp.where(atom_ref[s] < ATOMS, atom_ref[s], -1)
        own = jnp.where(row == s, atom.astype(F32), own)
    result = jnp.zeros((5 * SLOTS, 3 * LANES), F32)
    for tile, start in tiles:
        values = tile[start : start + SLOTS, :]
        high = values.astype(jnp.bfloat16)
        rest = values - high.astype(F32)
        middle = rest.astype(jnp.bfloat16)
        low = (rest - middle.astype(F32)).astype(jnp.bfloat16)
        same = [
            jnp.where(
                own[:, :SLOTS] == tile[start + SLOTS + k : start + SLOTS + k + 1, :SLOTS], 1.0, 0.0
            )
            for k in range(5)
        ]
        same = jnp.concatenate(same, axis=0).astype(jnp.bfloat16)
        result = result + jnp.dot(
            same, jnp.concatenate([high, middle, low], axis=1), preferred_element_type=F32
        )
    result = result[:, :LANES] + result[:, LANES : 2 * LANES] + result[:, 2 * LANES :]
    total = result[:SLOTS]
    for k in range(1, 5):
        total = total + pltpu.roll(result[SLOTS * k : SLOTS * (k + 1)], LANES - WIDTH * k, 1)
    return total


def finish(scale, local, before, after, two_up, two_down, own_block, proj_ref, strength_ref,
           offset_ref, atom_ref, work, table):
    weights = [scale * KINETIC / HALF_WIDTH * w for w in LAPLACE_COEFFS]
    table[...] = coefficients(
        ((own_block, 0), (before, X_ROWS), (after, X_ROWS), (two_up, 0), (two_down, 0)), atom_ref
    )
    work[:, REACH : CX - REACH] = local[:, REACH : CX - REACH]
    for o in range(ORB):
        for j in range(REACH):
            low = local[o, j]
            for i in range(j, REACH):
                rows = slice((o * REACH + i) * 32, (o * REACH + i + 1) * 32)
                low = low + weights[j + REACH - i] * before[rows, :].reshape(2, CY, LANES)
            work[o, j] = low
            high = local[o, CX - REACH + j]
            for i in range(j + 1):
                rows = slice((o * REACH + i) * 32, (o * REACH + i + 1) * 32)
                high = high + weights[REACH + i - j] * after[rows, :].reshape(2, CY, LANES)
            work[o, CX - REACH + j] = high

    lane = iota((1, 8, LANES), 2)

    def group_step(g, carry):
        rows = pl.ds(pl.multiple_of(g * 8, 8), 8)
        held = table[rows, :]
        added = [[None] * 8 for _ in range(ORB)]
        for p in range(NPROJ):
            strength = strength_ref[p] * (scale / HALF_WIDTH)
            spread = [
                jnp.broadcast_to(held[:, 2 * p + o : 2 * p + o + 1], (8, LANES)) * strength
                for o in range(ORB)
            ]
            for a in range(8):
                values = proj_ref[p, rows, LANES * a : LANES * (a + 1)]
                for o in range(ORB):
                    term = values * spread[o]
                    added[o][a] = term if p == 0 else added[o][a] + term
        patches = [swap_groups(jnp.stack(added[o])) for o in range(ORB)]
        for i in range(8):
            x, y, half, z = corner(offset_ref, g * 8 + i)
            shift = (z + LANES - 16 * i) % LANES
            moved = [pltpu.roll(patches[o], shift, 2) for o in range(ORB)]
            inside = (lane >= z) & (lane < z + 16)
            for o in range(ORB):
                place = (o, pl.ds(x, 8), half, pl.ds(y, 8), slice(None))
                work[place] = work[place] + jnp.where(inside, moved[o], 0.0)

            @pl.when(z > LANES - 16)
            def _():
                for o in range(ORB):
                    place = (o, pl.ds(x, 8), 1, pl.ds(y, 8), slice(None))
                    work[place] = work[place] + jnp.where(lane < z + 16 - LANES, moved[o], 0.0)

        return carry

    lax.fori_loop(0, SLOTS // 8, group_step, 0)


def unsplit(work, out):
    for half in range(2):
        out[:, :, :, LANES * half : LANES * (half + 1)] = work[:, :, half]


def middle_kernel(scale, local, before, after, two_up, two_down, own_block, proj_ref, strength_ref,
                  offset_ref, atom_ref, out, y_up, y_down, x_up, x_down, part, work, table):
    finish(scale, local, before, after, two_up, two_down, own_block, proj_ref, strength_ref,
           offset_ref, atom_ref, work, table)
    project(work, proj_ref, offset_ref, atom_ref, part)
    pack(work, part, y_up, y_down, x_up, x_down)
    unsplit(work, out)


def last_kernel(scale, local, before, after, two_up, two_down, own_block, proj_ref, strength_ref,
                offset_ref, atom_ref, out, work, table):
    finish(scale, local, before, after, two_up, two_down, own_block, proj_ref, strength_ref,
           offset_ref, atom_ref, work, table)
    unsplit(work, out)


def shaped(*shape):
    return jax.ShapeDtypeStruct(shape, F32)


PARAMS = pltpu.CompilerParams(vmem_limit_bytes=32 * 1024 * 1024)
FIELD = (ORB, CX, CY, NZ)
WORK = (ORB, CX, 2, CY, LANES)
SENT = (
    shaped(Y_ROWS + BLOCK, LANES),
    shaped(Y_ROWS + BLOCK, LANES),
    shaped(X_ROWS + BLOCK, LANES),
    shaped(X_ROWS + BLOCK, LANES),
    shaped(BLOCK, LANES),
)


def shift(value, axis, step):
    devices = lax.axis_size(axis)
    return lax.ppermute(value, axis, [(i, (i + step) % devices) for i in range(devices)])


def local_part(scale, field, potential, before, after, orbital):
    subtract = orbital is not None
    args = (field, potential, before, after) + ((orbital,) if subtract else ())

    def body(*refs):
        local_kernel(scale, subtract, *refs)

    return pl.pallas_call(
        body,
        out_shape=shaped(*WORK),
        in_specs=[VMEM] * len(args),
        out_specs=VMEM,
        scratch_shapes=[
            pltpu.VMEM((ORB, CX + 2 * REACH, 2, 32, LANES), F32),
            pltpu.VMEM((ORB * CX * CY, NZ), F32),
        ],
        compiler_params=PARAMS,
        name="local_part",
    )(*args)


def apply(scale, field, potential, sent, orbital, shared, last):
    y_up, y_down, x_up, x_down, part = sent
    projectors, strengths, offsets, atoms = shared
    y_before = shift(y_up, "gy", 1)
    y_after = shift(y_down, "gy", -1)
    y_two_before = shift(part, "gy", 2)
    y_two_after = shift(part, "gy", -2)
    tiles = (y_two_before, y_before[Y_ROWS:], part, y_after[Y_ROWS:], y_two_after)
    sums = jnp.concatenate(
        [tile[:SLOTS, :WIDTH] for tile in tiles] + [jnp.zeros((SLOTS, LANES - 5 * WIDTH), F32)],
        axis=1,
    )
    block = jnp.concatenate(
        [sums] + [tile[SLOTS : SLOTS + 1] for tile in tiles] + [tiles[0][SLOTS + 1 : SLOTS + 4]],
        axis=0,
    )
    x_up = lax.dynamic_update_slice(x_up, block, (X_ROWS, 0))
    x_down = lax.dynamic_update_slice(x_down, block, (X_ROWS, 0))
    x_before = shift(x_up, "gx", 1)
    x_after = shift(x_down, "gx", -1)
    x_two_before = shift(block, "gx", 2)
    x_two_after = shift(block, "gx", -2)
    local = local_part(scale, field, potential, y_before, y_after, orbital)
    kernel = last_kernel if last else middle_kernel

    def body(*refs):
        kernel(scale, *refs)

    return pl.pallas_call(
        body,
        out_shape=shaped(*FIELD) if last else (shaped(*FIELD),) + SENT,
        in_specs=[VMEM] * 7 + [SMEM] * 3,
        out_specs=VMEM if last else (VMEM,) * 6,
        scratch_shapes=[pltpu.VMEM(WORK, F32), pltpu.VMEM((SLOTS, LANES), F32)],
        compiler_params=PARAMS,
        name="last_part" if last else "middle_part",
    )(local, x_before, x_after, x_two_before, x_two_after, block, projectors, strengths, offsets, atoms)


def shards(orbitals, potential, projectors, strengths, atom_owner, slot_atom, slot_offset):
    projectors = jnp.transpose(projectors, (1, 0, 2))
    shared = (projectors, strengths, slot_offset, slot_atom)
    sent = pl.pallas_call(
        first_kernel,
        out_shape=SENT,
        in_specs=[VMEM, VMEM, SMEM, SMEM],
        out_specs=(VMEM,) * 5,
        scratch_shapes=[pltpu.VMEM(WORK, F32)],
        compiler_params=PARAMS,
        name="first_part",
    )(orbitals, projectors, slot_offset, slot_atom)
    first_filter, *sent = apply(1.0, orbitals, potential, sent, None, shared, False)
    second_filter = apply(2.0, first_filter, potential, sent, orbitals, shared, True)
    return (first_filter, second_filter)


def solution(mesh):
    return jax.shard_map(
        shards,
        mesh=mesh,
        in_specs=(
            P(None, "gx", "gy", None),
            P("gx", "gy", None),
            P(("gx", "gy"), None, None),
            P(),
            P(),
            P(("gx", "gy")),
            P(None, ("gx", "gy")),
        ),
        out_specs=(P(None, "gx", "gy", None), P(None, "gx", "gy", None)),
        check_vma=False,
    )
```

```python
import jax
import jax.numpy as jnp
from jax import lax
from jax.experimental import pallas as pl
from jax.experimental.pallas import tpu as pltpu
from jax.sharding import PartitionSpec as P

LAPLACE_COEFFS = (
    -5369.0 / 1800.0,
    12.0 / 7.0,
    -15.0 / 56.0,
    10.0 / 189.0,
    -1.0 / 112.0,
    2.0 / 1925.0,
    -1.0 / 16632.0,
)
SPACING = 0.4
CENTER = 45.0
HALF_WIDTH = 48.0
KINETIC = -0.5 / (SPACING * SPACING)
REACH = 6

ORB = 2
NPROJ = 9
LANES = 128
CX, CY, NZ = 32, 16, 256
SLOTS = 32
GROUPS = SLOTS // 8
ATOMS = 5120
WIDTH = 24
ATOM_LANE = 96
BLOCK = 8
COLUMN = 5 * BLOCK
PLANES = ORB * CX * 2
Y_ROWS = BLOCK + REACH * PLANES + 8
X_ROWS = ORB * REACH * 2 * CY

VMEM = pl.BlockSpec(memory_space=pltpu.VMEM)
SMEM = pl.BlockSpec(memory_space=pltpu.SMEM)
ANY = pl.BlockSpec(memory_space=pl.ANY)
HBM = pl.BlockSpec(memory_space=pltpu.HBM)
F32 = jnp.float32


def iota(shape, axis):
    return lax.broadcasted_iota(jnp.int32, shape, axis)


def swap_groups(x):
    row = iota((1, 8, LANES), 1)
    group = iota((1, 8, LANES), 2) // 16
    for d in (4, 2, 1):
        row_bit, group_bit = ((row & d) != 0, (group & d) != 0)
        later = pltpu.roll(pltpu.roll(x, 8 - d, 1), 16 * d, 2)
        if d == 4:
            other = later
        else:
            earlier = pltpu.roll(pltpu.roll(x, d, 1), LANES - 16 * d, 2)
            other = jnp.where(group_bit, later, earlier)
        x = jnp.where(row_bit == group_bit, x, other)
    return x


def corner(offset_ref, slot):
    z = offset_ref[2, slot]
    return offset_ref[0, slot], offset_ref[1, slot], z // LANES, z % LANES


def project(work, proj_ref, offset_ref, atom_ref, part):
    lane = iota((1, 8, LANES), 2)
    group_of_lane = lane // 16
    flat_lane = iota((BLOCK, LANES), 1)
    flat_row = iota((BLOCK, LANES), 0)
    block = jnp.zeros((BLOCK, LANES), F32)
    for s in range(SLOTS):
        place = (flat_row == s // 8) & (flat_lane == ATOM_LANE + s % 8)
        block = jnp.where(place, atom_ref[s].astype(F32), block)

    def group_step(g, block):
        patches = [jnp.zeros((8, 8, LANES), F32) for _ in range(ORB)]
        for i in range(8):
            x, y, half, z = corner(offset_ref, g * 8 + i)
            shift = (16 * i + LANES - z) % LANES
            for o in range(ORB):
                near = work[o, pl.ds(x, 8), half, pl.ds(y, 8), :]
                far = work[o, pl.ds(x, 8), 1, pl.ds(y, 8), :]
                window = pltpu.roll(jnp.where(lane >= z, near, far), shift, 2)
                patches[o] = jnp.where(group_of_lane == i, window, patches[o])
        patches = [swap_groups(patch) for patch in patches]
        tile = jnp.zeros((8, LANES), F32)
        rows = pl.ds(pl.multiple_of(g * 8, 8), 8)
        for p in range(NPROJ):
            values = [proj_ref[p, rows, LANES * a : LANES * (a + 1)] for a in range(8)]
            for o in range(ORB):
                total = values[0] * patches[o][0]
                for a in range(1, 8):
                    total = total + values[a] * patches[o][a]
                summed = jnp.sum(total, axis=1, keepdims=True)
                tile = jnp.where(flat_lane == 2 * p + o, summed, tile)
        return block + pltpu.roll(tile, g * WIDTH, 1)

    part[...] = lax.fori_loop(0, GROUPS, group_step, block, unroll=True)


def pack(work, part, y_up, y_down, x_up, x_down):
    for n in range(PLANES):
        o, x, half = (n // (2 * CX), n // 2 % CX, n % 2)
        y_down[BLOCK + REACH * n : BLOCK + REACH * n + 8, :] = work[o, x, half, 0:8, :]
    for n in reversed(range(PLANES)):
        o, x, half = (n // (2 * CX), n // 2 % CX, n % 2)
        y_up[REACH * (n + 1) : REACH * (n + 1) + 8, :] = work[o, x, half, 8:16, :]
    for target in (y_up, y_down):
        target[0:BLOCK, :] = part[...]
        target[Y_ROWS - 8 : Y_ROWS, :] = jnp.zeros((8, LANES), F32)
    for o in range(ORB):
        rows = slice(o * REACH * 32, (o + 1) * REACH * 32)
        x_up[rows, :] = work[o, CX - REACH : CX].reshape(REACH * 32, LANES)
        x_down[rows, :] = work[o, 0:REACH].reshape(REACH * 32, LANES)


def first_kernel(v, proj_hbm, offset_hbm, atom_hbm, y_up, y_down, x_up, x_down, part,
                 work, proj_ref, offset_ref, atom_ref, sems):
    copies = [
        pltpu.make_async_copy(offset_hbm, offset_ref, sems.at[0]),
        pltpu.make_async_copy(atom_hbm, atom_ref, sems.at[1]),
        pltpu.make_async_copy(v.at[:, :, :, 0:LANES], work.at[:, :, 0], sems.at[2]),
        pltpu.make_async_copy(v.at[:, :, :, LANES:NZ], work.at[:, :, 1], sems.at[3]),
        pltpu.make_async_copy(proj_hbm, proj_ref, sems.at[4]),
    ]
    for copy in copies:
        copy.start()
    for copy in copies:
        copy.wait()
    project(work, proj_ref, offset_ref, atom_ref, part)
    pack(work, part, y_up, y_down, x_up, x_down)


def local_kernel(scale, second, *refs):
    if second:
        field, potential, _, orbital, full, out, pad, along_z = refs
        halves = [field[:, :, half] for half in range(2)]
        for half in range(2):
            full[:, :, :, LANES * half : LANES * (half + 1)] = halves[half]
    else:
        field, potential, _, out, pad, along_z = refs
        halves = [field[:, :, :, LANES * half : LANES * (half + 1)] for half in range(2)]
    weights = [scale * KINETIC / HALF_WIDTH * w for w in LAPLACE_COEFFS]

    gap = jnp.abs(iota((NZ, NZ), 0) - iota((NZ, NZ), 1))
    band = jnp.zeros((NZ, NZ), F32)
    for r in range(1, REACH + 1):
        band = jnp.where(gap == r, weights[r], band)
    summed = None
    for half in range(2):
        term = jnp.dot(
            halves[half].reshape(ORB * CX * CY, LANES),
            band[LANES * half : LANES * (half + 1)],
            precision=lax.Precision.HIGHEST,
            preferred_element_type=F32,
        )
        summed = term if summed is None else summed + term
    along_z[...] = summed

    for o in range(ORB):
        for x in range(REACH):
            pad[o, x, :, 8:24, :] = jnp.zeros((2, CY, LANES), F32)
            pad[o, x + REACH + CX, :, 8:24, :] = jnp.zeros((2, CY, LANES), F32)
        pad[o, REACH : REACH + CX, :, 0:8, :] = jnp.zeros((CX, 2, 8, LANES), F32)
        pad[o, REACH : REACH + CX, :, 24:32, :] = jnp.zeros((CX, 2, 8, LANES), F32)
        for half in range(2):
            pad[o, REACH : REACH + CX, half, 8:24, :] = halves[half][o]

    def step(n, carry):
        o, x = (n // CX, n % CX)
        for half in range(2):
            lanes = slice(LANES * half, LANES * (half + 1))
            for t in range(2):
                rows = slice(8 + 8 * t, 16 + 8 * t)
                here = pad[o, x + REACH, half, rows, :]
                factor = potential[x, 8 * t : 8 * t + 8, lanes] * (scale / HALF_WIDTH) + (
                    3.0 * weights[0] - scale * CENTER / HALF_WIDTH
                )
                total = factor * here
                depth = pl.ds(pl.multiple_of(n * CY + 8 * t, 8), 8)
                total = total + along_z[depth, lanes]
                for r in range(1, REACH + 1):
                    paired = (
                        pad[o, x + REACH + r, half, rows, :] + pad[o, x + REACH - r, half, rows, :]
                    )
                    paired = paired + (
                        pad[o, x + REACH, half, 8 + 8 * t + r : 16 + 8 * t + r, :]
                        + pad[o, x + REACH, half, 8 + 8 * t - r : 16 + 8 * t - r, :]
                    )
                    total = total + weights[r] * paired
                if second:
                    total = total - orbital[o, x, 8 * t : 8 * t + 8, lanes]
                out[o, x, half, 8 * t : 8 * t + 8, :] = total
        return carry

    lax.fori_loop(0, ORB * CX, step, 0)


def edge_kernel(scale, before_ref, after_ref, local, out, before, after, sems):
    copies = [
        pltpu.make_async_copy(before_ref, before, sems.at[0]),
        pltpu.make_async_copy(after_ref, after, sems.at[1]),
    ]
    for copy in copies:
        copy.start()
    row = iota((8, LANES), 0)
    low, high = ([None], [None])
    for r in range(1, REACH + 1):
        weight = scale * KINETIC / HALF_WIDTH * LAPLACE_COEFFS[r]
        low.append(jnp.where(row < r, weight, 0.0).astype(F32))
        high.append(jnp.where(row >= 8 - r, weight, 0.0).astype(F32))
    for copy in copies:
        copy.wait()

    def step(n, carry):
        o, x = (n // CX, n % CX)
        for half in range(2):
            start = (n * 2 + half) * REACH
            first = local[o, x, half, 0:8, :]
            second = local[o, x, half, 8:16, :]
            for r in range(1, REACH + 1):
                first = first + low[r] * before[pl.ds(start + BLOCK + REACH - r, 8), :]
                second = second + high[r] * after[pl.ds(start + r, 8), :]
            out[o, x, half, 0:8, :] = first
            out[o, x, half, 8:16, :] = second
        return carry

    lax.fori_loop(0, ORB * CX, step, 0, unroll=4)


def gather_kernel(two_before, before, part, after, two_after, x_up_in, x_down_in, local,
                  x_up, x_down, column, sems):
    sources = (
        two_before,
        before.at[0:BLOCK],
        part,
        after.at[0:BLOCK],
        two_after,
    )
    copies = []
    for k, source in enumerate(sources):
        for n, (target, start) in enumerate(((x_up, X_ROWS), (x_down, X_ROWS), (column, 0))):
            rows = pl.ds(start + BLOCK * k, BLOCK)
            copies.append(pltpu.make_async_copy(source, target.at[rows], sems.at[3 * k + n]))
    for copy in copies:
        copy.start()
    for copy in copies:
        copy.wait()


def coefficients(columns, atom_ref):
    row = iota((8, LANES), 0)
    lane = iota((BLOCK, LANES), 1)
    own = []
    for g in range(GROUPS):
        held = jnp.full((8, LANES), -1.0, F32)
        for i in range(8):
            atom = atom_ref[8 * g + i]
            atom = jnp.where(atom < ATOMS, atom, -1)
            held = jnp.where(row == i, atom.astype(F32), held)
        own.append(held)
    own = jnp.concatenate(own, axis=0)
    result = jnp.zeros((GROUPS * SLOTS, 3 * LANES), F32)
    for values in columns:
        high = values.astype(jnp.bfloat16)
        rest = values - high.astype(F32)
        middle = rest.astype(jnp.bfloat16)
        low = (rest - middle.astype(F32)).astype(jnp.bfloat16)
        atoms = jnp.full((BLOCK, LANES), -2.0, F32)
        for k in range(5):
            tile = values[BLOCK * k : BLOCK * (k + 1)]
            moved = pltpu.roll(tile, LANES - ATOM_LANE + 8 * k, 1)
            atoms = jnp.where(lane // 8 == k, moved, atoms)
        same = jnp.concatenate(
            [jnp.where(own == atoms[g : g + 1, :], 1.0, 0.0) for g in range(GROUPS)], axis=0
        )
        same = same[:, :COLUMN].astype(jnp.bfloat16)
        result = result + jnp.dot(
            same, jnp.concatenate([high, middle, low], axis=1), preferred_element_type=F32
        )
    result = result[:, :LANES] + result[:, LANES : 2 * LANES] + result[:, 2 * LANES :]
    total = result[:SLOTS]
    for g in range(1, GROUPS):
        total = total + pltpu.roll(result[SLOTS * g : SLOTS * (g + 1)], LANES - WIDTH * g, 1)
    return total


def finish(scale, local, before_ref, after_ref, two_before, two_after, column, proj_ref,
           strength_ref, offset_ref, atom_ref, work, before, after, table, held, split, sems):
    weights = [scale * KINETIC / HALF_WIDTH * w for w in LAPLACE_COEFFS]
    copies = [
        pltpu.make_async_copy(before_ref, before, sems.at[0]),
        pltpu.make_async_copy(after_ref, after, sems.at[1]),
    ]
    for copy in copies:
        copy.start()
    work[:, REACH : CX - REACH] = local[:, REACH : CX - REACH]
    count = 0
    for s in range(SLOTS):
        split[count] = s
        z = offset_ref[2, s]
        count = count + jnp.where((z > LANES - 16) & (z < LANES), 1, 0)
    for copy in copies:
        copy.wait()
    table[...] = coefficients(
        (
            column[...],
            before[X_ROWS:, :],
            after[X_ROWS:, :],
            two_before[...],
            two_after[...],
        ),
        atom_ref,
    )
    for o in range(ORB):
        for j in range(REACH):
            low = local[o, j]
            for i in range(j, REACH):
                rows = slice((o * REACH + i) * 32, (o * REACH + i + 1) * 32)
                low = low + weights[j + REACH - i] * before[rows, :].reshape(2, CY, LANES)
            work[o, j] = low
            high = local[o, CX - REACH + j]
            for i in range(j + 1):
                rows = slice((o * REACH + i) * 32, (o * REACH + i + 1) * 32)
                high = high + weights[REACH + i - j] * after[rows, :].reshape(2, CY, LANES)
            work[o, CX - REACH + j] = high

    lane = iota((1, 8, LANES), 2)

    def group_step(g, carry):
        rows = pl.ds(pl.multiple_of(g * 8, 8), 8)
        factors = table[rows, :]
        added = [[None] * 8 for _ in range(ORB)]
        for p in range(NPROJ):
            strength = strength_ref[p] * (scale / HALF_WIDTH)
            spread = [
                jnp.broadcast_to(factors[:, 2 * p + o : 2 * p + o + 1], (8, LANES)) * strength
                for o in range(ORB)
            ]
            for a in range(8):
                values = proj_ref[p, rows, LANES * a : LANES * (a + 1)]
                for o in range(ORB):
                    term = values * spread[o]
                    added[o][a] = term if p == 0 else added[o][a] + term
        patches = [swap_groups(jnp.stack(added[o])) for o in range(ORB)]
        for o in range(ORB):
            held[g, o] = patches[o]
        for i in range(8):
            x, y, half, z = corner(offset_ref, g * 8 + i)
            shift = (z + LANES - 16 * i) % LANES
            inside = (lane >= z) & (lane < z + 16)
            places = [(o, pl.ds(x, 8), half, pl.ds(y, 8), slice(None)) for o in range(ORB)]
            sums = [
                work[places[o]] + jnp.where(inside, pltpu.roll(patches[o], shift, 2), 0.0)
                for o in range(ORB)
            ]
            for o in range(ORB):
                work[places[o]] = sums[o]
        return carry

    lax.fori_loop(0, GROUPS, group_step, 0, unroll=True)

    def split_step(n, carry):
        s = split[n]
        x, y, half, z = corner(offset_ref, s)
        shift = (z + LANES - 16 * (s % 8)) % LANES
        for o in range(ORB):
            place = (o, pl.ds(x, 8), 1, pl.ds(y, 8), slice(None))
            moved = pltpu.roll(held[s // 8, o], shift, 2)
            work[place] = work[place] + jnp.where(lane < z + 16 - LANES, moved, 0.0)
        return carry

    lax.fori_loop(0, count, split_step, 0)


def middle_kernel(scale, local, before_ref, after_ref, two_before, two_after, column, proj_ref,
                  strength_ref, offset_ref, atom_ref, work, y_up, y_down, x_up, x_down, part,
                  *scratch):
    finish(scale, local, before_ref, after_ref, two_before, two_after, column, proj_ref,
           strength_ref, offset_ref, atom_ref, work, *scratch)
    project(work, proj_ref, offset_ref, atom_ref, part)
    pack(work, part, y_up, y_down, x_up, x_down)


def last_kernel(scale, local, before_ref, after_ref, two_before, two_after, column, proj_ref,
                strength_ref, offset_ref, atom_ref, out, work, *scratch):
    finish(scale, local, before_ref, after_ref, two_before, two_after, column, proj_ref,
           strength_ref, offset_ref, atom_ref, work, *scratch)
    for half in range(2):
        out[:, :, :, LANES * half : LANES * (half + 1)] = work[:, :, half]


def shaped(*shape):
    return jax.ShapeDtypeStruct(shape, F32)


PARAMS = pltpu.CompilerParams(vmem_limit_bytes=16 * 1024 * 1024)
FIELD = (ORB, CX, CY, NZ)
WORK = (ORB, CX, 2, CY, LANES)
SENT = (
    shaped(Y_ROWS, LANES),
    shaped(Y_ROWS, LANES),
    shaped(X_ROWS + COLUMN, LANES),
    shaped(X_ROWS + COLUMN, LANES),
    shaped(BLOCK, LANES),
)


def cost(microseconds):
    return pl.CostEstimate(
        flops=0, transcendentals=0, bytes_accessed=int(microseconds * 3.0e6)
    )


def shift(value, axis, step):
    devices = lax.axis_size(axis)
    return lax.ppermute(value, axis, [(i, (i + step) % devices) for i in range(devices)])


def local_part(scale, field, potential, part, orbital):
    second = orbital is not None
    args = (field, potential, part) + ((orbital,) if second else ())

    def local_body(*refs):
        local_kernel(scale, second, *refs)

    return pl.pallas_call(
        local_body,
        out_shape=(shaped(*FIELD), shaped(*WORK)) if second else shaped(*WORK),
        in_specs=[VMEM, VMEM, ANY] + [VMEM] * (len(args) - 3),
        out_specs=(VMEM, VMEM) if second else VMEM,
        scratch_shapes=[
            pltpu.VMEM((ORB, CX + 2 * REACH, 2, 32, LANES), F32),
            pltpu.VMEM((ORB * CX * CY, NZ), F32),
        ],
        compiler_params=PARAMS,
        cost_estimate=cost(4),
        name="local_part",
    )(*args)


def edge_part(scale, before, after, local):
    def edge_body(*refs):
        edge_kernel(scale, *refs)

    return pl.pallas_call(
        edge_body,
        out_shape=shaped(*WORK),
        in_specs=[ANY, ANY, VMEM],
        out_specs=VMEM,
        scratch_shapes=[pltpu.VMEM((Y_ROWS, LANES), F32)] * 2 + [pltpu.SemaphoreType.DMA((2,))],
        compiler_params=PARAMS,
        cost_estimate=cost(2),
        name="edge_part",
    )(before, after, local)


def gather_part(two_before, before, part, after, two_after, x_up, x_down, local):
    return pl.pallas_call(
        gather_kernel,
        out_shape=(SENT[2], SENT[3], shaped(COLUMN, LANES)),
        in_specs=[ANY] * 8,
        out_specs=(ANY,) * 3,
        scratch_shapes=[pltpu.SemaphoreType.DMA((15,))],
        input_output_aliases={5: 0, 6: 1},
        compiler_params=PARAMS,
        cost_estimate=cost(1),
        name="gather_part",
    )(two_before, before, part, after, two_after, x_up, x_down, local)


def apply(scale, field, potential, sent, orbital, shared):
    second = orbital is not None
    y_up, y_down, x_up, x_down, part = sent
    projectors, strengths, offsets, atoms = shared
    y_before = shift(y_up, "gy", 1)
    y_after = shift(y_down, "gy", -1)
    y_two_before = shift(part, "gy", 2)
    y_two_after = shift(part, "gy", -2)
    local = local_part(scale, field, potential, part, orbital)
    if second:
        full, local = local
    x_up, x_down, column = gather_part(
        y_two_before, y_before, part, y_after, y_two_after, x_up, x_down, local
    )
    x_before = shift(x_up, "gx", 1)
    x_after = shift(x_down, "gx", -1)
    x_two_before = shift(column, "gx", 2)
    x_two_after = shift(column, "gx", -2)
    local = edge_part(scale, y_before, y_after, local)
    kernel = last_kernel if second else middle_kernel

    def end_body(*refs):
        kernel(scale, *refs)

    scratch = [
        pltpu.VMEM((X_ROWS + COLUMN, LANES), F32),
        pltpu.VMEM((X_ROWS + COLUMN, LANES), F32),
        pltpu.VMEM((SLOTS, LANES), F32),
        pltpu.VMEM((GROUPS, ORB, 8, 8, LANES), F32),
        pltpu.SMEM((SLOTS + 1,), jnp.int32),
        pltpu.SemaphoreType.DMA((2,)),
    ]
    result = pl.pallas_call(
        end_body,
        out_shape=shaped(*FIELD) if second else (shaped(*WORK),) + SENT,
        in_specs=[VMEM, ANY, ANY, VMEM, VMEM, VMEM, VMEM] + [SMEM] * 3,
        out_specs=VMEM if second else (VMEM,) * 6,
        scratch_shapes=([pltpu.VMEM(WORK, F32)] if second else []) + scratch,
        compiler_params=PARAMS,
        cost_estimate=cost(6),
        name="last_part" if second else "middle_part",
    )(local, x_before, x_after, x_two_before, x_two_after, column, projectors, strengths, offsets,
      atoms)
    return (full, result) if second else result


def shards(orbitals, potential, projectors, strengths, atom_owner, slot_atom, slot_offset):
    projectors = jnp.transpose(projectors, (1, 0, 2))
    shared = (projectors, strengths, slot_offset, slot_atom)
    sent = pl.pallas_call(
        first_kernel,
        out_shape=SENT,
        in_specs=[HBM] * 4,
        out_specs=(VMEM,) * 5,
        scratch_shapes=[
            pltpu.VMEM(WORK, F32),
            pltpu.VMEM((NPROJ, SLOTS, 8 * LANES), F32),
            pltpu.SMEM((3, SLOTS), jnp.int32),
            pltpu.SMEM((SLOTS,), jnp.int32),
            pltpu.SemaphoreType.DMA((5,)),
        ],
        compiler_params=PARAMS,
        cost_estimate=cost(3),
        name="first_part",
    )(orbitals, projectors, slot_offset, slot_atom)
    field, *sent = apply(1.0, orbitals, potential, sent, None, shared)
    return apply(2.0, field, potential, sent, orbitals, shared)


def solution(mesh):
    return jax.shard_map(
        shards,
        mesh=mesh,
        in_specs=(
            P(None, "gx", "gy", None),
            P("gx", "gy", None),
            P(("gx", "gy"), None, None),
            P(),
            P(),
            P(("gx", "gy")),
            P(None, ("gx", "gy")),
        ),
        out_specs=(P(None, "gx", "gy", None), P(None, "gx", "gy", None)),
        check_vma=False,
    )
```

```python
import jax
import jax.numpy as jnp
from jax import lax
from jax.experimental import pallas as pl
from jax.experimental.pallas import tpu as pltpu
from jax.sharding import PartitionSpec as P

LAPLACE_COEFFS = (
    -5369.0 / 1800.0,
    12.0 / 7.0,
    -15.0 / 56.0,
    10.0 / 189.0,
    -1.0 / 112.0,
    2.0 / 1925.0,
    -1.0 / 16632.0,
)
SPACING = 0.4
CENTER = 45.0
HALF_WIDTH = 48.0
KINETIC = -0.5 / (SPACING * SPACING)
REACH = 6

ORB = 2
NPROJ = 9
LANES = 128
CX, CY, NZ = 32, 16, 256
SLOTS = 32
GROUPS = SLOTS // 8
ATOMS = 5120
WIDTH = 24
ATOM_LANE = 96
BLOCK = 8
COLUMN = 5 * BLOCK
PLANES = ORB * CX * 2
Y_ROWS = BLOCK + REACH * PLANES + 8
X_ROWS = ORB * REACH * 2 * CY

VMEM = pl.BlockSpec(memory_space=pltpu.VMEM)
SMEM = pl.BlockSpec(memory_space=pltpu.SMEM)
ANY = pl.BlockSpec(memory_space=pl.ANY)
HBM = pl.BlockSpec(memory_space=pltpu.HBM)
F32 = jnp.float32


def iota(shape, axis):
    return lax.broadcasted_iota(jnp.int32, shape, axis)


def swap_list_row(tiles):
    row = iota((8, LANES), 0)
    for d in (1, 2, 4):
        first = (row & d) == 0
        new = list(tiles)
        for k in range(8):
            if k & d == 0:
                low, high = (tiles[k], tiles[k | d])
                new[k] = jnp.where(first, low, pltpu.roll(high, d, 0))
                new[k | d] = jnp.where(first, pltpu.roll(low, 8 - d, 0), high)
        tiles = new
    return tiles


def turned(tile, lanes):
    return pltpu.roll(tile, lanes % LANES, 1) if lanes % LANES else tile


def swap_list_group(tiles):
    group = iota((8, LANES), 1) // 16
    tiles = [turned(tile, 16 * k) for k, tile in enumerate(tiles)]
    tiles = [tiles[-k % 8] for k in range(8)]
    for d in (1, 2, 4):
        moved = (group & d) != 0
        tiles = [jnp.where(moved, tiles[(k - d) % 8], tiles[k]) for k in range(8)]
    return [turned(tile, -16 * k) for k, tile in enumerate(tiles)]


def swap_groups(x):
    tiles = swap_list_row([x[k] for k in range(8)])
    return jnp.stack(swap_list_row(swap_list_group(tiles)))


def corner(offset_ref, slot):
    z = offset_ref[2, slot]
    return offset_ref[0, slot], offset_ref[1, slot], z // LANES, z % LANES


def project(work, proj_ref, offset_ref, atom_ref, part):
    lane = iota((1, 8, LANES), 2)
    group_of_lane = lane // 16
    flat_lane = iota((BLOCK, LANES), 1)
    flat_row = iota((BLOCK, LANES), 0)
    block = jnp.zeros((BLOCK, LANES), F32)
    for s in range(SLOTS):
        place = (flat_row == s // 8) & (flat_lane == ATOM_LANE + s % 8)
        block = jnp.where(place, atom_ref[s].astype(F32), block)

    def group_step(g, block):
        patches = [jnp.zeros((8, 8, LANES), F32) for _ in range(ORB)]
        for i in range(8):
            x, y, half, z = corner(offset_ref, g * 8 + i)
            shift = (16 * i + LANES - z) % LANES
            for o in range(ORB):
                near = work[o, pl.ds(x, 8), half, pl.ds(y, 8), :]
                far = work[o, pl.ds(x, 8), 1, pl.ds(y, 8), :]
                window = pltpu.roll(jnp.where(lane >= z, near, far), shift, 2)
                patches[o] = jnp.where(group_of_lane == i, window, patches[o])
        patches = [swap_groups(patch) for patch in patches]
        tile = jnp.zeros((8, LANES), F32)
        rows = pl.ds(pl.multiple_of(g * 8, 8), 8)
        for p in range(NPROJ):
            values = [proj_ref[p, rows, LANES * a : LANES * (a + 1)] for a in range(8)]
            for o in range(ORB):
                total = values[0] * patches[o][0]
                for a in range(1, 8):
                    total = total + values[a] * patches[o][a]
                summed = jnp.sum(total, axis=1, keepdims=True)
                tile = jnp.where(flat_lane == 2 * p + o, summed, tile)
        return block + pltpu.roll(tile, g * WIDTH, 1)

    part[...] = lax.fori_loop(0, GROUPS, group_step, block, unroll=True)


def pack_y(work, part, up, down):
    for n in range(PLANES):
        o, x, half = (n // (2 * CX), n // 2 % CX, n % 2)
        down[BLOCK + REACH * n : BLOCK + REACH * n + 8, :] = work[o, x, half, 0:8, :]
    for n in reversed(range(PLANES)):
        o, x, half = (n // (2 * CX), n // 2 % CX, n % 2)
        up[REACH * (n + 1) : REACH * (n + 1) + 8, :] = work[o, x, half, 8:16, :]
    for target in (up, down):
        if part is not None:
            target[0:BLOCK, :] = part[...]
        target[Y_ROWS - 8 : Y_ROWS, :] = jnp.zeros((8, LANES), F32)


def pack_x(work, x_up, x_down):
    for o in range(ORB):
        rows = slice(o * REACH * 32, (o + 1) * REACH * 32)
        x_up[rows, :] = work[o, CX - REACH : CX].reshape(REACH * 32, LANES)
        x_down[rows, :] = work[o, 0:REACH].reshape(REACH * 32, LANES)


def is_odd():
    return lax.axis_index("gy") % 2


def first_kernel(v, proj_hbm, offset_hbm, atom_hbm, y_pair, y_next, x_up, x_down, part,
                 work, proj_ref, offset_ref, atom_ref, block, packed, xs_up, xs_down, sems):
    copies = [
        pltpu.make_async_copy(v.at[:, :, :, 0:LANES], work.at[:, :, 0], sems.at[0]),
        pltpu.make_async_copy(v.at[:, :, :, LANES:NZ], work.at[:, :, 1], sems.at[1]),
        pltpu.make_async_copy(offset_hbm, offset_ref, sems.at[2]),
        pltpu.make_async_copy(atom_hbm, atom_ref, sems.at[3]),
        pltpu.make_async_copy(proj_hbm, proj_ref, sems.at[4]),
    ]
    for copy in copies:
        copy.start()
    for copy in copies[:2]:
        copy.wait()
    pack_y(work, None, packed.at[0], packed.at[1])
    pack_x(work, xs_up, xs_down)
    odd = is_odd()
    halos = [
        pltpu.make_async_copy(
            source.at[pl.ds(start, rows)], target.at[pl.ds(start, rows)], sems.at[5 + k]
        )
        for k, (source, target, start, rows) in enumerate(
            (
                (packed.at[odd], y_pair, BLOCK, Y_ROWS - BLOCK),
                (packed.at[1 - odd], y_next, BLOCK, Y_ROWS - BLOCK),
                (xs_up, x_up, 0, X_ROWS),
                (xs_down, x_down, 0, X_ROWS),
            )
        )
    ]
    for copy in halos:
        copy.start()
    for copy in copies[2:]:
        copy.wait()
    project(work, proj_ref, offset_ref, atom_ref, block)
    blocks = [
        pltpu.make_async_copy(block, target.at[pl.ds(0, BLOCK)], sems.at[9 + k])
        for k, target in enumerate((y_pair, y_next, part))
    ]
    for copy in blocks:
        copy.start()
    for copy in halos + blocks:
        copy.wait()


def halves_of(field, split):
    if split:
        return [field[:, :, half] for half in range(2)]
    return [field[:, :, :, LANES * half : LANES * (half + 1)] for half in range(2)]


def local_kernel(scale, second, *refs):
    if second:
        field, potential, orbital, out, pad = refs
    else:
        field, potential, out, pad = refs
    halves = halves_of(field, second)
    weights = [scale * KINETIC / HALF_WIDTH * w for w in LAPLACE_COEFFS]
    for o in range(ORB):
        for x in range(REACH):
            pad[o, x, :, 8:24, :] = jnp.zeros((2, CY, LANES), F32)
            pad[o, x + REACH + CX, :, 8:24, :] = jnp.zeros((2, CY, LANES), F32)
        pad[o, REACH : REACH + CX, :, 0:8, :] = jnp.zeros((CX, 2, 8, LANES), F32)
        pad[o, REACH : REACH + CX, :, 24:32, :] = jnp.zeros((CX, 2, 8, LANES), F32)
        for half in range(2):
            pad[o, REACH : REACH + CX, half, 8:24, :] = halves[half][o]

    def step(n, carry):
        o, x = (n // CX, n % CX)
        for half in range(2):
            lanes = slice(LANES * half, LANES * (half + 1))
            for t in range(2):
                rows = slice(8 + 8 * t, 16 + 8 * t)
                here = pad[o, x + REACH, half, rows, :]
                factor = potential[x, 8 * t : 8 * t + 8, lanes] * (scale / HALF_WIDTH) + (
                    3.0 * weights[0] - scale * CENTER / HALF_WIDTH
                )
                total = factor * here
                for r in range(1, REACH + 1):
                    paired = (
                        pad[o, x + REACH + r, half, rows, :] + pad[o, x + REACH - r, half, rows, :]
                    )
                    paired = paired + (
                        pad[o, x + REACH, half, 8 + 8 * t + r : 16 + 8 * t + r, :]
                        + pad[o, x + REACH, half, 8 + 8 * t - r : 16 + 8 * t - r, :]
                    )
                    total = total + weights[r] * paired
                if second:
                    total = total - orbital[o, x, 8 * t : 8 * t + 8, lanes]
                out[o, x, half, 8 * t : 8 * t + 8, :] = total
        return carry

    lax.fori_loop(0, ORB * CX, step, 0)


def edge_kernel(scale, second, pair_ref, next_ref, local, field, *refs):
    if second:
        full, out, along_z, before, after, sems = refs
    else:
        out, along_z, before, after, sems = refs
    odd = is_odd()
    even_copies = [
        pltpu.make_async_copy(next_ref, before, sems.at[0]),
        pltpu.make_async_copy(pair_ref, after, sems.at[1]),
    ]
    odd_copies = [
        pltpu.make_async_copy(pair_ref, before, sems.at[0]),
        pltpu.make_async_copy(next_ref, after, sems.at[1]),
    ]

    @pl.when(odd == 0)
    def _():
        for copy in even_copies:
            copy.start()

    @pl.when(odd == 1)
    def _():
        for copy in odd_copies:
            copy.start()

    halves = halves_of(field, second)
    if second:
        for half in range(2):
            full[:, :, :, LANES * half : LANES * (half + 1)] = halves[half]
    gap = jnp.abs(iota((NZ, NZ), 0) - iota((NZ, NZ), 1))
    band = jnp.zeros((NZ, NZ), F32)
    for r in range(1, REACH + 1):
        weight = scale * KINETIC / HALF_WIDTH * LAPLACE_COEFFS[r]
        band = jnp.where(gap == r, weight, band)
    summed = None
    for half in range(2):
        term = jnp.dot(
            halves[half].reshape(ORB * CX * CY, LANES),
            band[LANES * half : LANES * (half + 1)],
            precision=lax.Precision.HIGHEST,
            preferred_element_type=F32,
        )
        summed = term if summed is None else summed + term
    along_z[...] = summed
    row = iota((8, LANES), 0)
    low, high = ([None], [None])
    for r in range(1, REACH + 1):
        weight = scale * KINETIC / HALF_WIDTH * LAPLACE_COEFFS[r]
        low.append(jnp.where(row < r, weight, 0.0).astype(F32))
        high.append(jnp.where(row >= 8 - r, weight, 0.0).astype(F32))

    @pl.when(odd == 0)
    def _():
        for copy in even_copies:
            copy.wait()

    @pl.when(odd == 1)
    def _():
        for copy in odd_copies:
            copy.wait()

    def step(n, carry):
        o, x = (n // CX, n % CX)
        depth = pl.multiple_of(n * CY, CY)
        for half in range(2):
            lanes = slice(LANES * half, LANES * (half + 1))
            start = (n * 2 + half) * REACH
            first = local[o, x, half, 0:8, :] + along_z[pl.ds(depth, 8), lanes]
            second_rows = local[o, x, half, 8:16, :] + along_z[pl.ds(depth + 8, 8), lanes]
            for r in range(1, REACH + 1):
                first = first + low[r] * before[pl.ds(start + BLOCK + REACH - r, 8), :]
                second_rows = second_rows + high[r] * after[pl.ds(start + r, 8), :]
            out[o, x, half, 0:8, :] = first
            out[o, x, half, 8:16, :] = second_rows
        return carry

    lax.fori_loop(0, ORB * CX, step, 0, unroll=4)


def gather_kernel(pair, after_pair, part, chips, after_chips, x_up_in, x_down_in, local,
                  x_up, x_down, column, sems):
    sources = (
        pair.at[0:BLOCK],
        after_pair.at[0:BLOCK],
        part,
        chips,
        after_chips,
    )
    copies = []
    for k, source in enumerate(sources):
        for n, (target, start) in enumerate(((x_up, X_ROWS), (x_down, X_ROWS), (column, 0))):
            rows = pl.ds(start + BLOCK * k, BLOCK)
            copies.append(pltpu.make_async_copy(source, target.at[rows], sems.at[3 * k + n]))
    for copy in copies:
        copy.start()
    for copy in copies:
        copy.wait()


def coefficients(columns, atom_ref):
    row = iota((8, LANES), 0)
    lane = iota((BLOCK, LANES), 1)
    own = []
    for g in range(GROUPS):
        held = jnp.full((8, LANES), -1.0, F32)
        for i in range(8):
            atom = atom_ref[8 * g + i]
            atom = jnp.where(atom < ATOMS, atom, -1)
            held = jnp.where(row == i, atom.astype(F32), held)
        own.append(held)
    own = jnp.concatenate(own, axis=0)
    result = jnp.zeros((GROUPS * SLOTS, 3 * LANES), F32)
    for values in columns:
        high = values.astype(jnp.bfloat16)
        rest = values - high.astype(F32)
        middle = rest.astype(jnp.bfloat16)
        low = (rest - middle.astype(F32)).astype(jnp.bfloat16)
        atoms = jnp.full((BLOCK, LANES), -2.0, F32)
        for k in range(5):
            tile = values[BLOCK * k : BLOCK * (k + 1)]
            moved = pltpu.roll(tile, LANES - ATOM_LANE + 8 * k, 1)
            atoms = jnp.where(lane // 8 == k, moved, atoms)
        same = jnp.concatenate(
            [jnp.where(own == atoms[g : g + 1, :], 1.0, 0.0) for g in range(GROUPS)], axis=0
        )
        same = same[:, :COLUMN].astype(jnp.bfloat16)
        result = result + jnp.dot(
            same, jnp.concatenate([high, middle, low], axis=1), preferred_element_type=F32
        )
    result = result[:, :LANES] + result[:, LANES : 2 * LANES] + result[:, 2 * LANES :]
    total = result[:SLOTS]
    for g in range(1, GROUPS):
        total = total + pltpu.roll(result[SLOTS * g : SLOTS * (g + 1)], LANES - WIDTH * g, 1)
    return total


def finish(scale, local, before_ref, after_ref, two_before, two_after, column, proj_ref,
           strength_ref, offset_ref, atom_ref, work, before, after, table, held, split, sems):
    weights = [scale * KINETIC / HALF_WIDTH * w for w in LAPLACE_COEFFS]
    copies = [
        pltpu.make_async_copy(before_ref, before, sems.at[0]),
        pltpu.make_async_copy(after_ref, after, sems.at[1]),
    ]
    for copy in copies:
        copy.start()
    work[:, REACH : CX - REACH] = local[:, REACH : CX - REACH]
    count = 0
    for s in range(SLOTS):
        split[count] = s
        z = offset_ref[2, s]
        count = count + jnp.where((z > LANES - 16) & (z < LANES), 1, 0)
    for copy in copies:
        copy.wait()
    table[...] = coefficients(
        (
            column[...],
            before[X_ROWS:, :],
            after[X_ROWS:, :],
            two_before[...],
            two_after[...],
        ),
        atom_ref,
    )
    for o in range(ORB):
        for j in range(REACH):
            low = local[o, j]
            for i in range(j, REACH):
                rows = slice((o * REACH + i) * 32, (o * REACH + i + 1) * 32)
                low = low + weights[j + REACH - i] * before[rows, :].reshape(2, CY, LANES)
            work[o, j] = low
            high = local[o, CX - REACH + j]
            for i in range(j + 1):
                rows = slice((o * REACH + i) * 32, (o * REACH + i + 1) * 32)
                high = high + weights[REACH + i - j] * after[rows, :].reshape(2, CY, LANES)
            work[o, CX - REACH + j] = high

    lane = iota((1, 8, LANES), 2)

    def group_step(g, carry):
        rows = pl.ds(pl.multiple_of(g * 8, 8), 8)
        factors = table[rows, :]
        added = [[None] * 8 for _ in range(ORB)]
        for p in range(NPROJ):
            strength = strength_ref[p] * (scale / HALF_WIDTH)
            spread = [
                jnp.broadcast_to(factors[:, 2 * p + o : 2 * p + o + 1], (8, LANES)) * strength
                for o in range(ORB)
            ]
            for a in range(8):
                values = proj_ref[p, rows, LANES * a : LANES * (a + 1)]
                for o in range(ORB):
                    term = values * spread[o]
                    added[o][a] = term if p == 0 else added[o][a] + term
        patches = [swap_groups(jnp.stack(added[o])) for o in range(ORB)]
        for o in range(ORB):
            held[g, o] = patches[o]
        for i in range(8):
            x, y, half, z = corner(offset_ref, g * 8 + i)
            shift = (z + LANES - 16 * i) % LANES
            inside = (lane >= z) & (lane < z + 16)
            places = [(o, pl.ds(x, 8), half, pl.ds(y, 8), slice(None)) for o in range(ORB)]
            sums = [
                work[places[o]] + jnp.where(inside, pltpu.roll(patches[o], shift, 2), 0.0)
                for o in range(ORB)
            ]
            for o in range(ORB):
                work[places[o]] = sums[o]
        return carry

    lax.fori_loop(0, GROUPS, group_step, 0, unroll=True)

    def split_step(n, carry):
        s = split[n]
        x, y, half, z = corner(offset_ref, s)
        shift = (z + LANES - 16 * (s % 8)) % LANES
        for o in range(ORB):
            place = (o, pl.ds(x, 8), 1, pl.ds(y, 8), slice(None))
            moved = pltpu.roll(held[s // 8, o], shift, 2)
            work[place] = work[place] + jnp.where(lane < z + 16 - LANES, moved, 0.0)
        return carry

    lax.fori_loop(0, count, split_step, 0)


def middle_kernel(scale, local, before_ref, after_ref, two_before, two_after, column, proj_ref,
                  strength_ref, offset_ref, atom_ref, work, y_pair, y_next, x_up, x_down, part,
                  *scratch):
    finish(scale, local, before_ref, after_ref, two_before, two_after, column, proj_ref,
           strength_ref, offset_ref, atom_ref, work, *scratch)
    project(work, proj_ref, offset_ref, atom_ref, part)
    pack_x(work, x_up, x_down)
    odd = is_odd()

    @pl.when(odd == 0)
    def _():
        pack_y(work, part, y_pair, y_next)

    @pl.when(odd == 1)
    def _():
        pack_y(work, part, y_next, y_pair)


def last_kernel(scale, local, before_ref, after_ref, two_before, two_after, column, proj_ref,
                strength_ref, offset_ref, atom_ref, out, work, *scratch):
    finish(scale, local, before_ref, after_ref, two_before, two_after, column, proj_ref,
           strength_ref, offset_ref, atom_ref, work, *scratch)
    for half in range(2):
        out[:, :, :, LANES * half : LANES * (half + 1)] = work[:, :, half]


def shaped(*shape):
    return jax.ShapeDtypeStruct(shape, F32)


PARAMS = pltpu.CompilerParams(vmem_limit_bytes=16 * 1024 * 1024)
FIELD = (ORB, CX, CY, NZ)
WORK = (ORB, CX, 2, CY, LANES)
SENT = (
    shaped(Y_ROWS, LANES),
    shaped(Y_ROWS, LANES),
    shaped(X_ROWS + COLUMN, LANES),
    shaped(X_ROWS + COLUMN, LANES),
    shaped(BLOCK, LANES),
)


def cost(microseconds):
    return pl.CostEstimate(
        flops=0, transcendentals=0, bytes_accessed=int(microseconds * 3.0e6)
    )


def shift(value, axis, step):
    devices = lax.axis_size(axis)
    return lax.ppermute(value, axis, [(i, (i + step) % devices) for i in range(devices)])


def swapped(value, span, later):
    devices = lax.axis_size("gy")
    pairs = []
    for i in range(devices):
        up = (i // span + later) % 2 == 0
        pairs.append((i, (i + (span if up else -span)) % devices))
    return lax.ppermute(value, "gy", pairs)


def local_part(scale, field, potential, orbital):
    second = orbital is not None
    args = (field, potential) + ((orbital,) if second else ())

    def local_body(*refs):
        local_kernel(scale, second, *refs)

    return pl.pallas_call(
        local_body,
        out_shape=shaped(*WORK),
        in_specs=[VMEM] * len(args),
        out_specs=VMEM,
        scratch_shapes=[pltpu.VMEM((ORB, CX + 2 * REACH, 2, 32, LANES), F32)],
        compiler_params=PARAMS,
        cost_estimate=cost(4),
        name="local_part",
    )(*args)


def edge_part(scale, before, after, local, field, second):
    def edge_body(*refs):
        edge_kernel(scale, second, *refs)

    return pl.pallas_call(
        edge_body,
        out_shape=(shaped(*FIELD), shaped(*WORK)) if second else shaped(*WORK),
        in_specs=[ANY, ANY, VMEM, VMEM],
        out_specs=(VMEM, VMEM) if second else VMEM,
        scratch_shapes=[pltpu.VMEM((ORB * CX * CY, NZ), F32)]
        + [pltpu.VMEM((Y_ROWS, LANES), F32)] * 2
        + [pltpu.SemaphoreType.DMA((2,))],
        compiler_params=PARAMS,
        cost_estimate=cost(2),
        name="edge_part",
    )(before, after, local, field)


def gather_part(pair, after_pair, part, chips, after_chips, x_up, x_down, local):
    return pl.pallas_call(
        gather_kernel,
        out_shape=(SENT[2], SENT[3], shaped(COLUMN, LANES)),
        in_specs=[ANY] * 8,
        out_specs=(ANY,) * 3,
        scratch_shapes=[pltpu.SemaphoreType.DMA((15,))],
        input_output_aliases={5: 0, 6: 1},
        compiler_params=PARAMS,
        cost_estimate=cost(1),
        name="gather_part",
    )(pair, after_pair, part, chips, after_chips, x_up, x_down, local)


def apply(scale, field, potential, sent, orbital, shared):
    second = orbital is not None
    y_pair, y_next, x_up, x_down, part = sent
    projectors, strengths, offsets, atoms = shared
    next_one = swapped(y_next, 1, 1)
    next_two = swapped(part, 2, 1)
    pair_two = swapped(part, 2, 0)
    pair_one = swapped(y_pair, 1, 0)
    if not second:
        field, part = lax.optimization_barrier((field, part))
    local = local_part(scale, field, potential, orbital)
    x_up, x_down, column = gather_part(
        pair_one, next_one, part, pair_two, next_two, x_up, x_down, local
    )
    x_before = shift(x_up, "gx", 1)
    x_after = shift(x_down, "gx", -1)
    x_two_before = shift(column, "gx", 2)
    x_two_after = shift(column, "gx", -2)
    local = edge_part(scale, pair_one, next_one, local, field, second)
    if second:
        full, local = local
    kernel = last_kernel if second else middle_kernel

    def end_body(*refs):
        kernel(scale, *refs)

    scratch = [
        pltpu.VMEM((X_ROWS + COLUMN, LANES), F32),
        pltpu.VMEM((X_ROWS + COLUMN, LANES), F32),
        pltpu.VMEM((SLOTS, LANES), F32),
        pltpu.VMEM((GROUPS, ORB, 8, 8, LANES), F32),
        pltpu.SMEM((SLOTS + 1,), jnp.int32),
        pltpu.SemaphoreType.DMA((2,)),
    ]
    result = pl.pallas_call(
        end_body,
        out_shape=shaped(*FIELD) if second else (shaped(*WORK),) + SENT,
        in_specs=[VMEM, ANY, ANY, VMEM, VMEM, VMEM, VMEM] + [SMEM] * 3,
        out_specs=VMEM if second else (VMEM,) * 6,
        scratch_shapes=([pltpu.VMEM(WORK, F32)] if second else []) + scratch,
        compiler_params=PARAMS,
        cost_estimate=cost(6),
        name="last_part" if second else "middle_part",
    )(local, x_before, x_after, x_two_before, x_two_after, column, projectors, strengths, offsets,
      atoms)
    return (full, result) if second else result


def shards(orbitals, potential, projectors, strengths, atom_owner, slot_atom, slot_offset):
    projectors = jnp.transpose(projectors, (1, 0, 2))
    shared = (projectors, strengths, slot_offset, slot_atom)
    sent = pl.pallas_call(
        first_kernel,
        out_shape=SENT,
        in_specs=[HBM] * 4,
        out_specs=(HBM,) * 5,
        scratch_shapes=[
            pltpu.VMEM(WORK, F32),
            pltpu.VMEM((NPROJ, SLOTS, 8 * LANES), F32),
            pltpu.SMEM((3, SLOTS), jnp.int32),
            pltpu.SMEM((SLOTS,), jnp.int32),
            pltpu.VMEM((BLOCK, LANES), F32),
            pltpu.VMEM((2, Y_ROWS, LANES), F32),
            pltpu.VMEM((X_ROWS, LANES), F32),
            pltpu.VMEM((X_ROWS, LANES), F32),
            pltpu.SemaphoreType.DMA((12,)),
        ],
        compiler_params=pltpu.CompilerParams(vmem_limit_bytes=60 * 1024 * 1024),
        cost_estimate=cost(3),
        name="first_part",
    )(orbitals, projectors, slot_offset, slot_atom)
    field, *sent = apply(1.0, orbitals, potential, sent, None, shared)
    return apply(2.0, field, potential, sent, orbitals, shared)


def solution(mesh):
    return jax.shard_map(
        shards,
        mesh=mesh,
        in_specs=(
            P(None, "gx", "gy", None),
            P("gx", "gy", None),
            P(("gx", "gy"), None, None),
            P(),
            P(),
            P(("gx", "gy")),
            P(None, ("gx", "gy")),
        ),
        out_specs=(P(None, "gx", "gy", None), P(None, "gx", "gy", None)),
        check_vma=False,
    )
```

```python
import jax
import jax.numpy as jnp
from jax import lax
from jax.experimental import pallas as pl
from jax.experimental.pallas import tpu as pltpu
from jax.sharding import PartitionSpec as P

LAPLACE_COEFFS = (
    -5369.0 / 1800.0,
    12.0 / 7.0,
    -15.0 / 56.0,
    10.0 / 189.0,
    -1.0 / 112.0,
    2.0 / 1925.0,
    -1.0 / 16632.0,
)
SPACING = 0.4
CENTER = 45.0
HALF_WIDTH = 48.0
KINETIC = -0.5 / (SPACING * SPACING)
REACH = 6

ORB = 2
NPROJ = 9
LANES = 128
CX, CY, NZ = 32, 16, 256
SLOTS = 32
GROUPS = SLOTS // 8
ATOMS = 5120
WIDTH = 24
ATOM_LANE = 96
BLOCK = 8
COLUMN = 5 * BLOCK
PLANES = ORB * CX * 2
Y_ROWS = BLOCK + REACH * PLANES + 8
X_ROWS = ORB * REACH * 2 * CY

VMEM = pl.BlockSpec(memory_space=pltpu.VMEM)
SMEM = pl.BlockSpec(memory_space=pltpu.SMEM)
ANY = pl.BlockSpec(memory_space=pl.ANY)
HBM = pl.BlockSpec(memory_space=pltpu.HBM)
F32 = jnp.float32


def iota(shape, axis):
    return lax.broadcasted_iota(jnp.int32, shape, axis)


def swap_list_row(tiles):
    row = iota((8, LANES), 0)
    for d in (1, 2, 4):
        first = (row & d) == 0
        new = list(tiles)
        for k in range(8):
            if k & d == 0:
                low, high = (tiles[k], tiles[k | d])
                new[k] = jnp.where(first, low, pltpu.roll(high, d, 0))
                new[k | d] = jnp.where(first, pltpu.roll(low, 8 - d, 0), high)
        tiles = new
    return tiles


def turned(tile, lanes):
    return pltpu.roll(tile, lanes % LANES, 1) if lanes % LANES else tile


def swap_list_group(tiles):
    group = iota((8, LANES), 1) // 16
    tiles = [turned(tile, 16 * k) for k, tile in enumerate(tiles)]
    tiles = [tiles[-k % 8] for k in range(8)]
    for d in (1, 2, 4):
        moved = (group & d) != 0
        tiles = [jnp.where(moved, tiles[(k - d) % 8], tiles[k]) for k in range(8)]
    return [turned(tile, -16 * k) for k, tile in enumerate(tiles)]


def swap_groups(x):
    tiles = swap_list_row([x[k] for k in range(8)])
    return jnp.stack(swap_list_row(swap_list_group(tiles)))


def corner(offset_ref, slot):
    z = offset_ref[2, slot]
    return offset_ref[0, slot], offset_ref[1, slot], z // LANES, z % LANES


def project(work, proj_ref, offset_ref, atom_ref, part):
    lane = iota((1, 8, LANES), 2)
    group_of_lane = lane // 16
    flat_lane = iota((BLOCK, LANES), 1)
    flat_row = iota((BLOCK, LANES), 0)
    block = jnp.zeros((BLOCK, LANES), F32)
    for s in range(SLOTS):
        place = (flat_row == s // 8) & (flat_lane == ATOM_LANE + s % 8)
        block = jnp.where(place, atom_ref[s].astype(F32), block)

    def group_step(g, block):
        patches = [jnp.zeros((8, 8, LANES), F32) for _ in range(ORB)]
        for i in range(8):
            x, y, half, z = corner(offset_ref, g * 8 + i)
            shift = (16 * i + LANES - z) % LANES
            for o in range(ORB):
                near = work[o, pl.ds(x, 8), half, pl.ds(y, 8), :]
                far = work[o, pl.ds(x, 8), 1, pl.ds(y, 8), :]
                window = pltpu.roll(jnp.where(lane >= z, near, far), shift, 2)
                patches[o] = jnp.where(group_of_lane == i, window, patches[o])
        patches = [swap_groups(patch) for patch in patches]
        tile = jnp.zeros((8, LANES), F32)
        rows = pl.ds(pl.multiple_of(g * 8, 8), 8)
        for p in range(NPROJ):
            values = [proj_ref[p, rows, LANES * a : LANES * (a + 1)] for a in range(8)]
            for o in range(ORB):
                total = values[0] * patches[o][0]
                for a in range(1, 8):
                    total = total + values[a] * patches[o][a]
                summed = jnp.sum(total, axis=1, keepdims=True)
                tile = jnp.where(flat_lane == 2 * p + o, summed, tile)
        return block + pltpu.roll(tile, g * WIDTH, 1)

    part[...] = lax.fori_loop(0, GROUPS, group_step, block, unroll=True)


def pack_y(work, part, up, down):
    for n in range(PLANES):
        o, x, half = (n // (2 * CX), n // 2 % CX, n % 2)
        down[BLOCK + REACH * n : BLOCK + REACH * n + 8, :] = work[o, x, half, 0:8, :]
    for n in reversed(range(PLANES)):
        o, x, half = (n // (2 * CX), n // 2 % CX, n % 2)
        up[REACH * (n + 1) : REACH * (n + 1) + 8, :] = work[o, x, half, 8:16, :]
    for target in (up, down):
        if part is not None:
            target[0:BLOCK, :] = part[...]
        target[Y_ROWS - 8 : Y_ROWS, :] = jnp.zeros((8, LANES), F32)


def pack_x(work, x_up, x_down):
    for o in range(ORB):
        rows = slice(o * REACH * 32, (o + 1) * REACH * 32)
        x_up[rows, :] = work[o, CX - REACH : CX].reshape(REACH * 32, LANES)
        x_down[rows, :] = work[o, 0:REACH].reshape(REACH * 32, LANES)


def is_odd():
    return lax.axis_index("gy") % 2


def first_kernel(v, proj_hbm, offset_hbm, atom_hbm, y_pair, y_next, x_up, x_down, part,
                 work, proj_ref, offset_ref, atom_ref, block, packed, xs_up, xs_down, sems):
    copies = [
        pltpu.make_async_copy(v.at[:, :, :, 0:LANES], work.at[:, :, 0], sems.at[0]),
        pltpu.make_async_copy(v.at[:, :, :, LANES:NZ], work.at[:, :, 1], sems.at[1]),
        pltpu.make_async_copy(offset_hbm, offset_ref, sems.at[2]),
        pltpu.make_async_copy(atom_hbm, atom_ref, sems.at[3]),
        pltpu.make_async_copy(proj_hbm, proj_ref, sems.at[4]),
    ]
    for copy in copies:
        copy.start()
    for copy in copies[:2]:
        copy.wait()
    pack_y(work, None, packed.at[0], packed.at[1])
    pack_x(work, xs_up, xs_down)
    odd = is_odd()
    halos = [
        pltpu.make_async_copy(
            source.at[pl.ds(start, rows)], target.at[pl.ds(start, rows)], sems.at[5 + k]
        )
        for k, (source, target, start, rows) in enumerate(
            (
                (packed.at[odd], y_pair, BLOCK, Y_ROWS - BLOCK),
                (packed.at[1 - odd], y_next, BLOCK, Y_ROWS - BLOCK),
                (xs_up, x_up, 0, X_ROWS),
                (xs_down, x_down, 0, X_ROWS),
            )
        )
    ]
    for copy in halos:
        copy.start()
    for copy in copies[2:]:
        copy.wait()
    project(work, proj_ref, offset_ref, atom_ref, block)
    blocks = [
        pltpu.make_async_copy(block, target.at[pl.ds(0, BLOCK)], sems.at[9 + k])
        for k, target in enumerate((y_pair, y_next, part))
    ]
    for copy in blocks:
        copy.start()
    for copy in halos + blocks:
        copy.wait()


def halves_of(field, split):
    if split:
        return [field[:, :, half] for half in range(2)]
    return [field[:, :, :, LANES * half : LANES * (half + 1)] for half in range(2)]


def local_kernel(scale, second, *refs):
    if second:
        field, potential, orbital, out, pad = refs
    else:
        field, potential, out, pad = refs
    halves = halves_of(field, second)
    weights = [scale * KINETIC / HALF_WIDTH * w for w in LAPLACE_COEFFS]
    for o in range(ORB):
        for x in range(REACH):
            pad[o, x, :, 8:24, :] = jnp.zeros((2, CY, LANES), F32)
            pad[o, x + REACH + CX, :, 8:24, :] = jnp.zeros((2, CY, LANES), F32)
        pad[o, REACH : REACH + CX, :, 0:8, :] = jnp.zeros((CX, 2, 8, LANES), F32)
        pad[o, REACH : REACH + CX, :, 24:32, :] = jnp.zeros((CX, 2, 8, LANES), F32)
        for half in range(2):
            pad[o, REACH : REACH + CX, half, 8:24, :] = halves[half][o]

    def step(n, carry):
        o, x = (n // (CX // 4), n % (CX // 4) * 4)
        for half in range(2):
            lanes = slice(LANES * half, LANES * (half + 1))
            for t in range(2):
                rows = slice(8 + 8 * t, 16 + 8 * t)
                line = [pad[o, x + k, half, rows, :] for k in range(4 + 2 * REACH)]
                for q in range(4):
                    factor = potential[x + q, 8 * t : 8 * t + 8, lanes] * (scale / HALF_WIDTH) + (
                        3.0 * weights[0] - scale * CENTER / HALF_WIDTH
                    )
                    middle = q + REACH
                    total = factor * line[middle]
                    for r in range(1, REACH + 1):
                        paired = line[middle + r] + line[middle - r]
                        paired = paired + (
                            pad[o, x + middle, half, 8 + 8 * t + r : 16 + 8 * t + r, :]
                            + pad[o, x + middle, half, 8 + 8 * t - r : 16 + 8 * t - r, :]
                        )
                        total = total + weights[r] * paired
                    if second:
                        total = total - orbital[o, x + q, 8 * t : 8 * t + 8, lanes]
                    out[o, x + q, half, 8 * t : 8 * t + 8, :] = total
        return carry

    lax.fori_loop(0, ORB * CX // 4, step, 0)


def edge_kernel(scale, second, pair_ref, next_ref, local, field, *refs):
    if second:
        full, out, along_z, before, after, sems = refs
    else:
        out, along_z, before, after, sems = refs
    odd = is_odd()
    even_copies = [
        pltpu.make_async_copy(next_ref, before, sems.at[0]),
        pltpu.make_async_copy(pair_ref, after, sems.at[1]),
    ]
    odd_copies = [
        pltpu.make_async_copy(pair_ref, before, sems.at[0]),
        pltpu.make_async_copy(next_ref, after, sems.at[1]),
    ]

    @pl.when(odd == 0)
    def _():
        for copy in even_copies:
            copy.start()

    @pl.when(odd == 1)
    def _():
        for copy in odd_copies:
            copy.start()

    halves = halves_of(field, second)
    if second:
        fulls = [
            pltpu.make_async_copy(
                field.at[:, :, half],
                full.at[:, :, :, LANES * half : LANES * (half + 1)],
                sems.at[2 + half],
            )
            for half in range(2)
        ]
        for copy in fulls:
            copy.start()
    gap = jnp.abs(iota((NZ, NZ), 0) - iota((NZ, NZ), 1))
    band = jnp.zeros((NZ, NZ), F32)
    for r in range(1, REACH + 1):
        weight = scale * KINETIC / HALF_WIDTH * LAPLACE_COEFFS[r]
        band = jnp.where(gap == r, weight, band)
    values = jnp.concatenate(
        [half.reshape(ORB * CX * CY, LANES) for half in halves], axis=1
    )
    value_high = values.astype(jnp.bfloat16)
    value_low = (values - value_high.astype(F32)).astype(jnp.bfloat16)
    band_high = band.astype(jnp.bfloat16)
    band_low = (band - band_high.astype(F32)).astype(jnp.bfloat16)
    summed = jnp.dot(value_high, band_high, preferred_element_type=F32)
    summed = summed + jnp.dot(value_low, band_high, preferred_element_type=F32)
    summed = summed + jnp.dot(value_high, band_low, preferred_element_type=F32)
    along_z[...] = summed
    row = iota((8, LANES), 0)
    low, high = ([None], [None])
    for r in range(1, REACH + 1):
        weight = scale * KINETIC / HALF_WIDTH * LAPLACE_COEFFS[r]
        low.append(jnp.where(row < r, weight, 0.0).astype(F32))
        high.append(jnp.where(row >= 8 - r, weight, 0.0).astype(F32))

    @pl.when(odd == 0)
    def _():
        for copy in even_copies:
            copy.wait()

    @pl.when(odd == 1)
    def _():
        for copy in odd_copies:
            copy.wait()

    def step(n, carry):
        o, x = (n // CX, n % CX)
        depth = pl.multiple_of(n * CY, CY)
        for half in range(2):
            lanes = slice(LANES * half, LANES * (half + 1))
            start = (n * 2 + half) * REACH
            first = local[o, x, half, 0:8, :] + along_z[pl.ds(depth, 8), lanes]
            second_rows = local[o, x, half, 8:16, :] + along_z[pl.ds(depth + 8, 8), lanes]
            for r in range(1, REACH + 1):
                first = first + low[r] * before[pl.ds(start + BLOCK + REACH - r, 8), :]
                second_rows = second_rows + high[r] * after[pl.ds(start + r, 8), :]
            out[o, x, half, 0:8, :] = first
            out[o, x, half, 8:16, :] = second_rows
        return carry

    lax.fori_loop(0, ORB * CX, step, 0, unroll=4)
    if second:
        for copy in fulls:
            copy.wait()


def gather_kernel(pair, after_pair, part, chips, after_chips, x_up_in, x_down_in, local,
                  x_up, x_down, column, sems):
    sources = (
        pair.at[0:BLOCK],
        after_pair.at[0:BLOCK],
        part,
        chips,
        after_chips,
    )
    copies = []
    for k, source in enumerate(sources):
        for n, (target, start) in enumerate(((x_up, X_ROWS), (x_down, X_ROWS), (column, 0))):
            rows = pl.ds(start + BLOCK * k, BLOCK)
            copies.append(pltpu.make_async_copy(source, target.at[rows], sems.at[3 * k + n]))
    for copy in copies:
        copy.start()
    for copy in copies:
        copy.wait()


def coefficients(columns, atom_ref):
    row = iota((8, LANES), 0)
    lane = iota((BLOCK, LANES), 1)
    own = []
    for g in range(GROUPS):
        held = jnp.full((8, LANES), -1.0, F32)
        for i in range(8):
            atom = atom_ref[8 * g + i]
            atom = jnp.where(atom < ATOMS, atom, -1)
            held = jnp.where(row == i, atom.astype(F32), held)
        own.append(held)
    own = jnp.concatenate(own, axis=0)
    result = jnp.zeros((GROUPS * SLOTS, 3 * LANES), F32)
    for values in columns:
        high = values.astype(jnp.bfloat16)
        rest = values - high.astype(F32)
        middle = rest.astype(jnp.bfloat16)
        low = (rest - middle.astype(F32)).astype(jnp.bfloat16)
        atoms = jnp.full((BLOCK, LANES), -2.0, F32)
        for k in range(5):
            tile = values[BLOCK * k : BLOCK * (k + 1)]
            moved = pltpu.roll(tile, LANES - ATOM_LANE + 8 * k, 1)
            atoms = jnp.where(lane // 8 == k, moved, atoms)
        same = jnp.concatenate(
            [jnp.where(own == atoms[g : g + 1, :], 1.0, 0.0) for g in range(GROUPS)], axis=0
        )
        same = same[:, :COLUMN].astype(jnp.bfloat16)
        result = result + jnp.dot(
            same, jnp.concatenate([high, middle, low], axis=1), preferred_element_type=F32
        )
    result = result[:, :LANES] + result[:, LANES : 2 * LANES] + result[:, 2 * LANES :]
    total = result[:SLOTS]
    for g in range(1, GROUPS):
        total = total + pltpu.roll(result[SLOTS * g : SLOTS * (g + 1)], LANES - WIDTH * g, 1)
    return total


def finish(scale, local, before, after, two_before, two_after, column, proj_ref,
           strength_ref, offset_ref, atom_ref, work, table, held, split):
    weights = [scale * KINETIC / HALF_WIDTH * w for w in LAPLACE_COEFFS]
    work[:, REACH : CX - REACH] = local[:, REACH : CX - REACH]
    count = 0
    for s in range(SLOTS):
        split[count] = s
        z = offset_ref[2, s]
        count = count + jnp.where((z > LANES - 16) & (z < LANES), 1, 0)
    table[...] = coefficients(
        (
            column[...],
            before[X_ROWS:, :],
            after[X_ROWS:, :],
            two_before[...],
            two_after[...],
        ),
        atom_ref,
    )
    for o in range(ORB):
        for j in range(REACH):
            low = local[o, j]
            for i in range(j, REACH):
                rows = slice((o * REACH + i) * 32, (o * REACH + i + 1) * 32)
                low = low + weights[j + REACH - i] * before[rows, :].reshape(2, CY, LANES)
            work[o, j] = low
            high = local[o, CX - REACH + j]
            for i in range(j + 1):
                rows = slice((o * REACH + i) * 32, (o * REACH + i + 1) * 32)
                high = high + weights[REACH + i - j] * after[rows, :].reshape(2, CY, LANES)
            work[o, CX - REACH + j] = high

    lane = iota((1, 8, LANES), 2)

    def group_step(g, carry):
        rows = pl.ds(pl.multiple_of(g * 8, 8), 8)
        factors = table[rows, :]
        added = [[None] * 8 for _ in range(ORB)]
        for p in range(NPROJ):
            strength = strength_ref[p] * (scale / HALF_WIDTH)
            spread = [
                jnp.broadcast_to(factors[:, 2 * p + o : 2 * p + o + 1], (8, LANES)) * strength
                for o in range(ORB)
            ]
            for a in range(8):
                values = proj_ref[p, rows, LANES * a : LANES * (a + 1)]
                for o in range(ORB):
                    term = values * spread[o]
                    added[o][a] = term if p == 0 else added[o][a] + term
        patches = [swap_groups(jnp.stack(added[o])) for o in range(ORB)]
        for o in range(ORB):
            held[g, o] = patches[o]
        for i in range(8):
            x, y, half, z = corner(offset_ref, g * 8 + i)
            shift = (z + LANES - 16 * i) % LANES
            inside = (lane >= z) & (lane < z + 16)
            places = [(o, pl.ds(x, 8), half, pl.ds(y, 8), slice(None)) for o in range(ORB)]
            sums = [
                work[places[o]] + jnp.where(inside, pltpu.roll(patches[o], shift, 2), 0.0)
                for o in range(ORB)
            ]
            for o in range(ORB):
                work[places[o]] = sums[o]
        return carry

    lax.fori_loop(0, GROUPS, group_step, 0, unroll=True)

    def split_step(n, carry):
        s = split[n]
        x, y, half, z = corner(offset_ref, s)
        shift = (z + LANES - 16 * (s % 8)) % LANES
        for o in range(ORB):
            place = (o, pl.ds(x, 8), 1, pl.ds(y, 8), slice(None))
            moved = pltpu.roll(held[s // 8, o], shift, 2)
            work[place] = work[place] + jnp.where(lane < z + 16 - LANES, moved, 0.0)
        return carry

    lax.fori_loop(0, count, split_step, 0)


def middle_kernel(scale, local, before_ref, after_ref, two_before, two_after, column, proj_ref,
                  strength_ref, offset_ref, atom_ref, work, y_pair, y_next, x_up, x_down, part,
                  *scratch):
    finish(scale, local, before_ref, after_ref, two_before, two_after, column, proj_ref,
           strength_ref, offset_ref, atom_ref, work, *scratch)
    project(work, proj_ref, offset_ref, atom_ref, part)
    pack_x(work, x_up, x_down)
    odd = is_odd()

    @pl.when(odd == 0)
    def _():
        pack_y(work, part, y_pair, y_next)

    @pl.when(odd == 1)
    def _():
        pack_y(work, part, y_next, y_pair)


def last_kernel(scale, local, before_ref, after_ref, two_before, two_after, column, proj_ref,
                strength_ref, offset_ref, atom_ref, out, work, *scratch):
    finish(scale, local, before_ref, after_ref, two_before, two_after, column, proj_ref,
           strength_ref, offset_ref, atom_ref, work, *scratch)
    for half in range(2):
        out[:, :, :, LANES * half : LANES * (half + 1)] = work[:, :, half]


def shaped(*shape):
    return jax.ShapeDtypeStruct(shape, F32)


PARAMS = pltpu.CompilerParams(vmem_limit_bytes=16 * 1024 * 1024)
FIELD = (ORB, CX, CY, NZ)
WORK = (ORB, CX, 2, CY, LANES)
SENT = (
    shaped(Y_ROWS, LANES),
    shaped(Y_ROWS, LANES),
    shaped(X_ROWS + COLUMN, LANES),
    shaped(X_ROWS + COLUMN, LANES),
    shaped(BLOCK, LANES),
)


def cost(microseconds):
    return pl.CostEstimate(
        flops=0, transcendentals=0, bytes_accessed=int(microseconds * 3.0e6)
    )


def shift(value, axis, step):
    devices = lax.axis_size(axis)
    return lax.ppermute(value, axis, [(i, (i + step) % devices) for i in range(devices)])


def swapped(value, span, later):
    devices = lax.axis_size("gy")
    pairs = []
    for i in range(devices):
        up = (i // span + later) % 2 == 0
        pairs.append((i, (i + (span if up else -span)) % devices))
    return lax.ppermute(value, "gy", pairs)


def local_part(scale, field, potential, orbital):
    second = orbital is not None
    args = (field, potential) + ((orbital,) if second else ())

    def local_body(*refs):
        local_kernel(scale, second, *refs)

    return pl.pallas_call(
        local_body,
        out_shape=shaped(*WORK),
        in_specs=[VMEM] * len(args),
        out_specs=VMEM,
        scratch_shapes=[pltpu.VMEM((ORB, CX + 2 * REACH, 2, 32, LANES), F32)],
        compiler_params=PARAMS,
        cost_estimate=cost(4),
        name="local_part",
    )(*args)


def edge_part(scale, before, after, local, field, second):
    def edge_body(*refs):
        edge_kernel(scale, second, *refs)

    return pl.pallas_call(
        edge_body,
        out_shape=(shaped(*FIELD), shaped(*WORK)) if second else shaped(*WORK),
        in_specs=[ANY, ANY, VMEM, VMEM],
        out_specs=(HBM, VMEM) if second else VMEM,
        scratch_shapes=[pltpu.VMEM((ORB * CX * CY, NZ), F32)]
        + [pltpu.VMEM((Y_ROWS, LANES), F32)] * 2
        + [pltpu.SemaphoreType.DMA((4,))],
        compiler_params=PARAMS,
        cost_estimate=cost(2),
        name="edge_part",
    )(before, after, local, field)


def gather_part(pair, after_pair, part, chips, after_chips, x_up, x_down, local):
    return pl.pallas_call(
        gather_kernel,
        out_shape=(SENT[2], SENT[3], shaped(COLUMN, LANES)),
        in_specs=[ANY] * 8,
        out_specs=(ANY,) * 3,
        scratch_shapes=[pltpu.SemaphoreType.DMA((15,))],
        input_output_aliases={5: 0, 6: 1},
        compiler_params=PARAMS,
        cost_estimate=cost(1),
        name="gather_part",
    )(pair, after_pair, part, chips, after_chips, x_up, x_down, local)


def apply(scale, field, potential, sent, orbital, shared):
    second = orbital is not None
    y_pair, y_next, x_up, x_down, part = sent
    projectors, strengths, offsets, atoms = shared
    next_one = swapped(y_next, 1, 1)
    next_two = swapped(part, 2, 1)
    pair_two = swapped(part, 2, 0)
    pair_one = swapped(y_pair, 1, 0)
    if not second:
        field, part = lax.optimization_barrier((field, part))
    local = local_part(scale, field, potential, orbital)
    x_up, x_down, column = gather_part(
        pair_one, next_one, part, pair_two, next_two, x_up, x_down, local
    )
    x_before = shift(x_up, "gx", 1)
    x_after = shift(x_down, "gx", -1)
    x_two_before = shift(column, "gx", 2)
    x_two_after = shift(column, "gx", -2)
    local = edge_part(scale, pair_one, next_one, local, field, second)
    if second:
        full, local = local
    kernel = last_kernel if second else middle_kernel

    def end_body(*refs):
        kernel(scale, *refs)

    scratch = [
        pltpu.VMEM((SLOTS, LANES), F32),
        pltpu.VMEM((GROUPS, ORB, 8, 8, LANES), F32),
        pltpu.SMEM((SLOTS + 1,), jnp.int32),
    ]
    result = pl.pallas_call(
        end_body,
        out_shape=shaped(*FIELD) if second else (shaped(*WORK),) + SENT,
        in_specs=[VMEM] * 7 + [SMEM] * 3,
        out_specs=VMEM if second else (VMEM,) * 6,
        scratch_shapes=([pltpu.VMEM(WORK, F32)] if second else []) + scratch,
        compiler_params=PARAMS,
        cost_estimate=cost(6),
        name="last_part" if second else "middle_part",
    )(local, x_before, x_after, x_two_before, x_two_after, column, projectors, strengths, offsets,
      atoms)
    return (full, result) if second else result


def shards(orbitals, potential, projectors, strengths, atom_owner, slot_atom, slot_offset):
    projectors = jnp.transpose(projectors, (1, 0, 2))
    shared = (projectors, strengths, slot_offset, slot_atom)
    sent = pl.pallas_call(
        first_kernel,
        out_shape=SENT,
        in_specs=[HBM] * 4,
        out_specs=(HBM,) * 5,
        scratch_shapes=[
            pltpu.VMEM(WORK, F32),
            pltpu.VMEM((NPROJ, SLOTS, 8 * LANES), F32),
            pltpu.SMEM((3, SLOTS), jnp.int32),
            pltpu.SMEM((SLOTS,), jnp.int32),
            pltpu.VMEM((BLOCK, LANES), F32),
            pltpu.VMEM((2, Y_ROWS, LANES), F32),
            pltpu.VMEM((X_ROWS, LANES), F32),
            pltpu.VMEM((X_ROWS, LANES), F32),
            pltpu.SemaphoreType.DMA((12,)),
        ],
        compiler_params=pltpu.CompilerParams(vmem_limit_bytes=60 * 1024 * 1024),
        cost_estimate=cost(3),
        name="first_part",
    )(orbitals, projectors, slot_offset, slot_atom)
    field, *sent = apply(1.0, orbitals, potential, sent, None, shared)
    return apply(2.0, field, potential, sent, orbitals, shared)


def solution(mesh):
    return jax.shard_map(
        shards,
        mesh=mesh,
        in_specs=(
            P(None, "gx", "gy", None),
            P("gx", "gy", None),
            P(("gx", "gy"), None, None),
            P(),
            P(),
            P(("gx", "gy")),
            P(None, ("gx", "gy")),
        ),
        out_specs=(P(None, "gx", "gy", None), P(None, "gx", "gy", None)),
        check_vma=False,
    )
```

```python
import jax
import jax.numpy as jnp
from jax import lax
from jax.experimental import pallas as pl
from jax.experimental.pallas import tpu as pltpu
from jax.sharding import PartitionSpec as P

LAPLACE_COEFFS = (
    -5369.0 / 1800.0,
    12.0 / 7.0,
    -15.0 / 56.0,
    10.0 / 189.0,
    -1.0 / 112.0,
    2.0 / 1925.0,
    -1.0 / 16632.0,
)
SPACING = 0.4
CENTER = 45.0
HALF_WIDTH = 48.0
KINETIC = -0.5 / (SPACING * SPACING)
REACH = 6

ORB = 2
NPROJ = 9
LANES = 128
CX, CY, NZ = 32, 16, 256
SLOTS = 32
GROUPS = SLOTS // 8
ATOMS = 5120
WIDTH = 24
ATOM_LANE = 96
BLOCK = 8
COLUMN = 5 * BLOCK
PLANES = ORB * CX * 2
Y_ROWS = BLOCK + REACH * PLANES + 8
X_ROWS = ORB * REACH * 2 * CY

VMEM = pl.BlockSpec(memory_space=pltpu.VMEM)
SMEM = pl.BlockSpec(memory_space=pltpu.SMEM)
ANY = pl.BlockSpec(memory_space=pl.ANY)
HBM = pl.BlockSpec(memory_space=pltpu.HBM)
F32 = jnp.float32


def iota(shape, axis):
    return lax.broadcasted_iota(jnp.int32, shape, axis)


def swap_list_row(tiles):
    row = iota((8, LANES), 0)
    for d in (1, 2, 4):
        first = (row & d) == 0
        new = list(tiles)
        for k in range(8):
            if k & d == 0:
                low, high = (tiles[k], tiles[k | d])
                new[k] = jnp.where(first, low, pltpu.roll(high, d, 0))
                new[k | d] = jnp.where(first, pltpu.roll(low, 8 - d, 0), high)
        tiles = new
    return tiles


def turned(tile, lanes):
    return pltpu.roll(tile, lanes % LANES, 1) if lanes % LANES else tile


def swap_list_group(tiles):
    group = iota((8, LANES), 1) // 16
    tiles = [turned(tile, 16 * k) for k, tile in enumerate(tiles)]
    tiles = [tiles[-k % 8] for k in range(8)]
    for d in (1, 2, 4):
        moved = (group & d) != 0
        tiles = [jnp.where(moved, tiles[(k - d) % 8], tiles[k]) for k in range(8)]
    return [turned(tile, -16 * k) for k, tile in enumerate(tiles)]


def swap_groups(x):
    tiles = swap_list_row([x[k] for k in range(8)])
    return jnp.stack(swap_list_row(swap_list_group(tiles)))


def corner(offset_ref, slot):
    z = offset_ref[2, slot]
    return offset_ref[0, slot], offset_ref[1, slot], z // LANES, z % LANES


def rotate(work, rotated):
    for o in range(ORB):
        for x in range(CX):
            for half in range(2):
                for t in range(2):
                    rows = slice(8 * t, 8 * t + 8)
                    rotated[o, x, half, rows, :] = turned(work[o, x, half, rows, :], 16 * (x % 8))


def project(rotated, proj_ref, offset_ref, atom_ref, part):
    flat_lane = iota((BLOCK, LANES), 1)
    flat_row = iota((BLOCK, LANES), 0)
    block = jnp.zeros((BLOCK, LANES), F32)
    for s in range(SLOTS):
        place = (flat_row == s // 8) & (flat_lane == ATOM_LANE + s % 8)
        block = jnp.where(place, atom_ref[s].astype(F32), block)

    for g in range(GROUPS):
        slots = [[None] * 8 for _ in range(ORB)]
        for i in range(8):
            x, y, half, z = corner(offset_ref, g * 8 + i)
            place = flat_lane + (LANES - z)
            window = (place // 16 - x) & 7
            near = place % 16 < LANES - z
            shift = (4 * LANES + LANES - z - 16 * x) % LANES
            for o in range(ORB):
                low = rotated[o, x, half, pl.ds(y, 8), :]
                high = rotated[o, x, 1, pl.ds(y, 8), :]
                for a in range(1, 8):
                    here = window == a
                    low = jnp.where(here, rotated[o, x + a, half, pl.ds(y, 8), :], low)
                    high = jnp.where(here, rotated[o, x + a, 1, pl.ds(y, 8), :], high)
                slots[o][i] = pltpu.roll(jnp.where(near, low, high), shift, 1)
        patches = [swap_list_group(swap_list_row(tiles)) for tiles in slots]
        tile = jnp.zeros((8, LANES), F32)
        rows = slice(8 * g, 8 * g + 8)
        for p in range(NPROJ):
            values = [proj_ref[p, rows, LANES * a : LANES * (a + 1)] for a in range(8)]
            for o in range(ORB):
                total = values[0] * patches[o][0]
                for a in range(1, 8):
                    total = total + values[a] * patches[o][a]
                summed = jnp.sum(total, axis=1, keepdims=True)
                tile = jnp.where(flat_lane == 2 * p + o, summed, tile)
        block = block + turned(tile, g * WIDTH)

    part[...] = block


def pack_y(work, part, up, down):
    for n in range(PLANES):
        o, x, half = (n // (2 * CX), n // 2 % CX, n % 2)
        down[BLOCK + REACH * n : BLOCK + REACH * n + 8, :] = work[o, x, half, 0:8, :]
    for n in reversed(range(PLANES)):
        o, x, half = (n // (2 * CX), n // 2 % CX, n % 2)
        up[REACH * (n + 1) : REACH * (n + 1) + 8, :] = work[o, x, half, 8:16, :]
    for target in (up, down):
        if part is not None:
            target[0:BLOCK, :] = part[...]
        target[Y_ROWS - 8 : Y_ROWS, :] = jnp.zeros((8, LANES), F32)


def pack_x(work, x_up, x_down):
    for o in range(ORB):
        rows = slice(o * REACH * 32, (o + 1) * REACH * 32)
        x_up[rows, :] = work[o, CX - REACH : CX].reshape(REACH * 32, LANES)
        x_down[rows, :] = work[o, 0:REACH].reshape(REACH * 32, LANES)


def is_odd():
    return lax.axis_index("gy") % 2


def first_kernel(v, proj_hbm, offset_hbm, atom_hbm, y_pair, y_next, x_up, x_down, part,
                 work, rotated, proj_ref, offset_ref, atom_ref, block, packed, xs_up, xs_down,
                 sems):
    copies = [
        pltpu.make_async_copy(v.at[:, :, :, 0:LANES], work.at[:, :, 0], sems.at[0]),
        pltpu.make_async_copy(v.at[:, :, :, LANES:NZ], work.at[:, :, 1], sems.at[1]),
        pltpu.make_async_copy(offset_hbm, offset_ref, sems.at[2]),
        pltpu.make_async_copy(atom_hbm, atom_ref, sems.at[3]),
        pltpu.make_async_copy(proj_hbm, proj_ref, sems.at[4]),
    ]
    for copy in copies:
        copy.start()
    for copy in copies[:2]:
        copy.wait()
    pack_y(work, None, packed.at[0], packed.at[1])
    pack_x(work, xs_up, xs_down)
    odd = is_odd()
    halos = [
        pltpu.make_async_copy(
            source.at[pl.ds(start, rows)], target.at[pl.ds(start, rows)], sems.at[5 + k]
        )
        for k, (source, target, start, rows) in enumerate(
            (
                (packed.at[odd], y_pair, BLOCK, Y_ROWS - BLOCK),
                (packed.at[1 - odd], y_next, BLOCK, Y_ROWS - BLOCK),
                (xs_up, x_up, 0, X_ROWS),
                (xs_down, x_down, 0, X_ROWS),
            )
        )
    ]
    for copy in halos:
        copy.start()
    rotate(work, rotated)
    for copy in copies[2:]:
        copy.wait()
    project(rotated, proj_ref, offset_ref, atom_ref, block)
    blocks = [
        pltpu.make_async_copy(block, target.at[pl.ds(0, BLOCK)], sems.at[9 + k])
        for k, target in enumerate((y_pair, y_next, part))
    ]
    for copy in blocks:
        copy.start()
    for copy in halos + blocks:
        copy.wait()


def halves_of(field, split):
    if split:
        return [field[:, :, half] for half in range(2)]
    return [field[:, :, :, LANES * half : LANES * (half + 1)] for half in range(2)]


def local_kernel(scale, second, *refs):
    if second:
        field, potential, orbital, out, pad = refs
    else:
        field, potential, out, pad = refs
    halves = halves_of(field, second)
    weights = [scale * KINETIC / HALF_WIDTH * w for w in LAPLACE_COEFFS]
    for o in range(ORB):
        for x in range(REACH):
            pad[o, x, :, 8:24, :] = jnp.zeros((2, CY, LANES), F32)
            pad[o, x + REACH + CX, :, 8:24, :] = jnp.zeros((2, CY, LANES), F32)
        pad[o, REACH : REACH + CX, :, 0:8, :] = jnp.zeros((CX, 2, 8, LANES), F32)
        pad[o, REACH : REACH + CX, :, 24:32, :] = jnp.zeros((CX, 2, 8, LANES), F32)
        for half in range(2):
            pad[o, REACH : REACH + CX, half, 8:24, :] = halves[half][o]

    def step(n, carry):
        o, x = (n // (CX // 4), n % (CX // 4) * 4)
        for half in range(2):
            lanes = slice(LANES * half, LANES * (half + 1))
            for t in range(2):
                rows = slice(8 + 8 * t, 16 + 8 * t)
                line = [pad[o, x + k, half, rows, :] for k in range(4 + 2 * REACH)]
                for q in range(4):
                    factor = potential[x + q, 8 * t : 8 * t + 8, lanes] * (scale / HALF_WIDTH) + (
                        3.0 * weights[0] - scale * CENTER / HALF_WIDTH
                    )
                    middle = q + REACH
                    total = factor * line[middle]
                    for r in range(1, REACH + 1):
                        paired = line[middle + r] + line[middle - r]
                        paired = paired + (
                            pad[o, x + middle, half, 8 + 8 * t + r : 16 + 8 * t + r, :]
                            + pad[o, x + middle, half, 8 + 8 * t - r : 16 + 8 * t - r, :]
                        )
                        total = total + weights[r] * paired
                    if second:
                        total = total - orbital[o, x + q, 8 * t : 8 * t + 8, lanes]
                    out[o, x + q, half, 8 * t : 8 * t + 8, :] = total
        return carry

    lax.fori_loop(0, ORB * CX // 4, step, 0)


def edge_kernel(scale, second, pair_ref, next_ref, local, field, *refs):
    if second:
        full, out, along_z, before, after, sems = refs
    else:
        out, along_z, before, after, sems = refs
    odd = is_odd()
    even_copies = [
        pltpu.make_async_copy(next_ref, before, sems.at[0]),
        pltpu.make_async_copy(pair_ref, after, sems.at[1]),
    ]
    odd_copies = [
        pltpu.make_async_copy(pair_ref, before, sems.at[0]),
        pltpu.make_async_copy(next_ref, after, sems.at[1]),
    ]

    @pl.when(odd == 0)
    def _():
        for copy in even_copies:
            copy.start()

    @pl.when(odd == 1)
    def _():
        for copy in odd_copies:
            copy.start()

    halves = halves_of(field, second)
    if second:
        fulls = [
            pltpu.make_async_copy(
                field.at[:, :, half],
                full.at[:, :, :, LANES * half : LANES * (half + 1)],
                sems.at[2 + half],
            )
            for half in range(2)
        ]
        for copy in fulls:
            copy.start()
    gap = jnp.abs(iota((NZ, NZ), 0) - iota((NZ, NZ), 1))
    band = jnp.zeros((NZ, NZ), F32)
    for r in range(1, REACH + 1):
        weight = scale * KINETIC / HALF_WIDTH * LAPLACE_COEFFS[r]
        band = jnp.where(gap == r, weight, band)
    values = jnp.concatenate(
        [half.reshape(ORB * CX * CY, LANES) for half in halves], axis=1
    )
    value_high = values.astype(jnp.bfloat16)
    value_low = (values - value_high.astype(F32)).astype(jnp.bfloat16)
    band_high = band.astype(jnp.bfloat16)
    band_low = (band - band_high.astype(F32)).astype(jnp.bfloat16)
    summed = jnp.dot(value_high, band_high, preferred_element_type=F32)
    summed = summed + jnp.dot(value_low, band_high, preferred_element_type=F32)
    summed = summed + jnp.dot(value_high, band_low, preferred_element_type=F32)
    along_z[...] = summed
    row = iota((8, LANES), 0)
    low, high = ([None], [None])
    for r in range(1, REACH + 1):
        weight = scale * KINETIC / HALF_WIDTH * LAPLACE_COEFFS[r]
        low.append(jnp.where(row < r, weight, 0.0).astype(F32))
        high.append(jnp.where(row >= 8 - r, weight, 0.0).astype(F32))

    @pl.when(odd == 0)
    def _():
        for copy in even_copies:
            copy.wait()

    @pl.when(odd == 1)
    def _():
        for copy in odd_copies:
            copy.wait()

    def step(n, carry):
        o, x = (n // CX, n % CX)
        depth = pl.multiple_of(n * CY, CY)
        for half in range(2):
            lanes = slice(LANES * half, LANES * (half + 1))
            start = (n * 2 + half) * REACH
            first = local[o, x, half, 0:8, :] + along_z[pl.ds(depth, 8), lanes]
            second_rows = local[o, x, half, 8:16, :] + along_z[pl.ds(depth + 8, 8), lanes]
            for r in range(1, REACH + 1):
                first = first + low[r] * before[pl.ds(start + BLOCK + REACH - r, 8), :]
                second_rows = second_rows + high[r] * after[pl.ds(start + r, 8), :]
            out[o, x, half, 0:8, :] = first
            out[o, x, half, 8:16, :] = second_rows
        return carry

    lax.fori_loop(0, ORB * CX, step, 0, unroll=4)
    if second:
        for copy in fulls:
            copy.wait()


def gather_kernel(pair, after_pair, part, chips, after_chips, x_up_in, x_down_in, local,
                  x_up, x_down, column, sems):
    sources = (
        pair.at[0:BLOCK],
        after_pair.at[0:BLOCK],
        part,
        chips,
        after_chips,
    )
    copies = []
    for k, source in enumerate(sources):
        for n, (target, start) in enumerate(((x_up, X_ROWS), (x_down, X_ROWS), (column, 0))):
            rows = pl.ds(start + BLOCK * k, BLOCK)
            copies.append(pltpu.make_async_copy(source, target.at[rows], sems.at[3 * k + n]))
    for copy in copies:
        copy.start()
    for copy in copies:
        copy.wait()


def coefficients(columns, atom_ref):
    row = iota((8, LANES), 0)
    lane = iota((BLOCK, LANES), 1)
    own = []
    for g in range(GROUPS):
        held = jnp.full((8, LANES), -1.0, F32)
        for i in range(8):
            atom = atom_ref[8 * g + i]
            atom = jnp.where(atom < ATOMS, atom, -1)
            held = jnp.where(row == i, atom.astype(F32), held)
        own.append(held)
    own = jnp.concatenate(own, axis=0)
    result = jnp.zeros((GROUPS * SLOTS, 3 * LANES), F32)
    for values in columns:
        high = values.astype(jnp.bfloat16)
        rest = values - high.astype(F32)
        middle = rest.astype(jnp.bfloat16)
        low = (rest - middle.astype(F32)).astype(jnp.bfloat16)
        atoms = jnp.full((BLOCK, LANES), -2.0, F32)
        for k in range(5):
            tile = values[BLOCK * k : BLOCK * (k + 1)]
            moved = pltpu.roll(tile, LANES - ATOM_LANE + 8 * k, 1)
            atoms = jnp.where(lane // 8 == k, moved, atoms)
        same = jnp.concatenate(
            [jnp.where(own == atoms[g : g + 1, :], 1.0, 0.0) for g in range(GROUPS)], axis=0
        )
        same = same[:, :COLUMN].astype(jnp.bfloat16)
        result = result + jnp.dot(
            same, jnp.concatenate([high, middle, low], axis=1), preferred_element_type=F32
        )
    result = result[:, :LANES] + result[:, LANES : 2 * LANES] + result[:, 2 * LANES :]
    total = result[:SLOTS]
    for g in range(1, GROUPS):
        total = total + pltpu.roll(result[SLOTS * g : SLOTS * (g + 1)], LANES - WIDTH * g, 1)
    return total


def finish(scale, local, before, after, two_before, two_after, column, proj_ref,
           strength_ref, offset_ref, atom_ref, work, table, held, split):
    weights = [scale * KINETIC / HALF_WIDTH * w for w in LAPLACE_COEFFS]
    work[:, REACH : CX - REACH] = local[:, REACH : CX - REACH]
    count = 0
    for s in range(SLOTS):
        split[count] = s
        z = offset_ref[2, s]
        count = count + jnp.where((z > LANES - 16) & (z < LANES), 1, 0)
    table[...] = coefficients(
        (
            column[...],
            before[X_ROWS:, :],
            after[X_ROWS:, :],
            two_before[...],
            two_after[...],
        ),
        atom_ref,
    )
    for o in range(ORB):
        for j in range(REACH):
            low = local[o, j]
            for i in range(j, REACH):
                rows = slice((o * REACH + i) * 32, (o * REACH + i + 1) * 32)
                low = low + weights[j + REACH - i] * before[rows, :].reshape(2, CY, LANES)
            work[o, j] = low
            high = local[o, CX - REACH + j]
            for i in range(j + 1):
                rows = slice((o * REACH + i) * 32, (o * REACH + i + 1) * 32)
                high = high + weights[REACH + i - j] * after[rows, :].reshape(2, CY, LANES)
            work[o, CX - REACH + j] = high

    lane = iota((1, 8, LANES), 2)

    def group_step(g, carry):
        rows = pl.ds(pl.multiple_of(g * 8, 8), 8)
        factors = table[rows, :]
        added = [[None] * 8 for _ in range(ORB)]
        for p in range(NPROJ):
            strength = strength_ref[p] * (scale / HALF_WIDTH)
            spread = [
                jnp.broadcast_to(factors[:, 2 * p + o : 2 * p + o + 1], (8, LANES)) * strength
                for o in range(ORB)
            ]
            for a in range(8):
                values = proj_ref[p, rows, LANES * a : LANES * (a + 1)]
                for o in range(ORB):
                    term = values * spread[o]
                    added[o][a] = term if p == 0 else added[o][a] + term
        patches = [swap_groups(jnp.stack(added[o])) for o in range(ORB)]
        for o in range(ORB):
            held[g, o] = patches[o]
        for i in range(8):
            x, y, half, z = corner(offset_ref, g * 8 + i)
            shift = (z + LANES - 16 * i) % LANES
            inside = (lane >= z) & (lane < z + 16)
            places = [(o, pl.ds(x, 8), half, pl.ds(y, 8), slice(None)) for o in range(ORB)]
            sums = [
                work[places[o]] + jnp.where(inside, pltpu.roll(patches[o], shift, 2), 0.0)
                for o in range(ORB)
            ]
            for o in range(ORB):
                work[places[o]] = sums[o]
        return carry

    lax.fori_loop(0, GROUPS, group_step, 0, unroll=True)

    def split_step(n, carry):
        s = split[n]
        x, y, half, z = corner(offset_ref, s)
        shift = (z + LANES - 16 * (s % 8)) % LANES
        for o in range(ORB):
            place = (o, pl.ds(x, 8), 1, pl.ds(y, 8), slice(None))
            moved = pltpu.roll(held[s // 8, o], shift, 2)
            work[place] = work[place] + jnp.where(lane < z + 16 - LANES, moved, 0.0)
        return carry

    lax.fori_loop(0, count, split_step, 0)


def middle_kernel(scale, local, before_ref, after_ref, two_before, two_after, column, proj_ref,
                  strength_ref, offset_ref, atom_ref, work, y_pair, y_next, x_up, x_down, part,
                  rotated, *scratch):
    finish(scale, local, before_ref, after_ref, two_before, two_after, column, proj_ref,
           strength_ref, offset_ref, atom_ref, work, *scratch)
    rotate(work, rotated)
    project(rotated, proj_ref, offset_ref, atom_ref, part)
    pack_x(work, x_up, x_down)
    odd = is_odd()

    @pl.when(odd == 0)
    def _():
        pack_y(work, part, y_pair, y_next)

    @pl.when(odd == 1)
    def _():
        pack_y(work, part, y_next, y_pair)


def last_kernel(scale, local, before_ref, after_ref, two_before, two_after, column, proj_ref,
                strength_ref, offset_ref, atom_ref, out, work, *scratch):
    *scratch, sems = scratch
    finish(scale, local, before_ref, after_ref, two_before, two_after, column, proj_ref,
           strength_ref, offset_ref, atom_ref, work, *scratch)
    copies = [
        pltpu.make_async_copy(
            work.at[:, :, half], out.at[:, :, :, LANES * half : LANES * (half + 1)], sems.at[half]
        )
        for half in range(2)
    ]
    for copy in copies:
        copy.start()
    for copy in copies:
        copy.wait()


def shaped(*shape):
    return jax.ShapeDtypeStruct(shape, F32)


PARAMS = pltpu.CompilerParams(vmem_limit_bytes=16 * 1024 * 1024)
FIELD = (ORB, CX, CY, NZ)
WORK = (ORB, CX, 2, CY, LANES)
SENT = (
    shaped(Y_ROWS, LANES),
    shaped(Y_ROWS, LANES),
    shaped(X_ROWS + COLUMN, LANES),
    shaped(X_ROWS + COLUMN, LANES),
    shaped(BLOCK, LANES),
)


def cost(microseconds):
    return pl.CostEstimate(
        flops=0, transcendentals=0, bytes_accessed=int(microseconds * 3.0e6)
    )


def shift(value, axis, step):
    devices = lax.axis_size(axis)
    return lax.ppermute(value, axis, [(i, (i + step) % devices) for i in range(devices)])


def swapped(value, span, later):
    devices = lax.axis_size("gy")
    pairs = []
    for i in range(devices):
        up = (i // span + later) % 2 == 0
        pairs.append((i, (i + (span if up else -span)) % devices))
    return lax.ppermute(value, "gy", pairs)


def local_part(scale, field, potential, orbital):
    second = orbital is not None
    args = (field, potential) + ((orbital,) if second else ())

    def local_body(*refs):
        local_kernel(scale, second, *refs)

    return pl.pallas_call(
        local_body,
        out_shape=shaped(*WORK),
        in_specs=[VMEM] * len(args),
        out_specs=VMEM,
        scratch_shapes=[pltpu.VMEM((ORB, CX + 2 * REACH, 2, 32, LANES), F32)],
        compiler_params=PARAMS,
        cost_estimate=cost(4),
        name="local_part",
    )(*args)


def edge_part(scale, before, after, local, field, second):
    def edge_body(*refs):
        edge_kernel(scale, second, *refs)

    return pl.pallas_call(
        edge_body,
        out_shape=(shaped(*FIELD), shaped(*WORK)) if second else shaped(*WORK),
        in_specs=[ANY, ANY, VMEM, VMEM],
        out_specs=(HBM, VMEM) if second else VMEM,
        scratch_shapes=[pltpu.VMEM((ORB * CX * CY, NZ), F32)]
        + [pltpu.VMEM((Y_ROWS, LANES), F32)] * 2
        + [pltpu.SemaphoreType.DMA((4,))],
        compiler_params=PARAMS,
        cost_estimate=cost(2),
        name="edge_part",
    )(before, after, local, field)


def gather_part(pair, after_pair, part, chips, after_chips, x_up, x_down, local):
    return pl.pallas_call(
        gather_kernel,
        out_shape=(SENT[2], SENT[3], shaped(COLUMN, LANES)),
        in_specs=[ANY] * 8,
        out_specs=(ANY,) * 3,
        scratch_shapes=[pltpu.SemaphoreType.DMA((15,))],
        input_output_aliases={5: 0, 6: 1},
        compiler_params=PARAMS,
        cost_estimate=cost(1),
        name="gather_part",
    )(pair, after_pair, part, chips, after_chips, x_up, x_down, local)


def apply(scale, field, potential, sent, orbital, shared):
    second = orbital is not None
    y_pair, y_next, x_up, x_down, part = sent
    projectors, strengths, offsets, atoms = shared
    next_one = swapped(y_next, 1, 1)
    next_two = swapped(part, 2, 1)
    pair_two = swapped(part, 2, 0)
    pair_one = swapped(y_pair, 1, 0)
    if not second:
        field, part = lax.optimization_barrier((field, part))
    local = local_part(scale, field, potential, orbital)
    x_up, x_down, column = gather_part(
        pair_one, next_one, part, pair_two, next_two, x_up, x_down, local
    )
    x_before = shift(x_up, "gx", 1)
    x_after = shift(x_down, "gx", -1)
    x_two_before = shift(column, "gx", 2)
    x_two_after = shift(column, "gx", -2)
    local = edge_part(scale, pair_one, next_one, local, field, second)
    if second:
        full, local = local
    kernel = last_kernel if second else middle_kernel

    def end_body(*refs):
        kernel(scale, *refs)

    scratch = [
        pltpu.VMEM((SLOTS, LANES), F32),
        pltpu.VMEM((GROUPS, ORB, 8, 8, LANES), F32),
        pltpu.SMEM((SLOTS + 1,), jnp.int32),
    ]
    result = pl.pallas_call(
        end_body,
        out_shape=shaped(*FIELD) if second else (shaped(*WORK),) + SENT,
        in_specs=[VMEM] * 7 + [SMEM] * 3,
        out_specs=HBM if second else (VMEM,) * 6,
        scratch_shapes=[pltpu.VMEM(WORK, F32)]
        + scratch
        + ([pltpu.SemaphoreType.DMA((2,))] if second else []),
        compiler_params=PARAMS,
        cost_estimate=cost(6),
        name="last_part" if second else "middle_part",
    )(local, x_before, x_after, x_two_before, x_two_after, column, projectors, strengths, offsets,
      atoms)
    return (full, result) if second else result


def shards(orbitals, potential, projectors, strengths, atom_owner, slot_atom, slot_offset):
    projectors = jnp.transpose(projectors, (1, 0, 2))
    shared = (projectors, strengths, slot_offset, slot_atom)
    sent = pl.pallas_call(
        first_kernel,
        out_shape=SENT,
        in_specs=[HBM] * 4,
        out_specs=(HBM,) * 5,
        scratch_shapes=[
            pltpu.VMEM(WORK, F32),
            pltpu.VMEM(WORK, F32),
            pltpu.VMEM((NPROJ, SLOTS, 8 * LANES), F32),
            pltpu.SMEM((3, SLOTS), jnp.int32),
            pltpu.SMEM((SLOTS,), jnp.int32),
            pltpu.VMEM((BLOCK, LANES), F32),
            pltpu.VMEM((2, Y_ROWS, LANES), F32),
            pltpu.VMEM((X_ROWS, LANES), F32),
            pltpu.VMEM((X_ROWS, LANES), F32),
            pltpu.SemaphoreType.DMA((12,)),
        ],
        compiler_params=pltpu.CompilerParams(vmem_limit_bytes=60 * 1024 * 1024),
        cost_estimate=cost(3),
        name="first_part",
    )(orbitals, projectors, slot_offset, slot_atom)
    field, *sent = apply(1.0, orbitals, potential, sent, None, shared)
    return apply(2.0, field, potential, sent, orbitals, shared)


def solution(mesh):
    return jax.shard_map(
        shards,
        mesh=mesh,
        in_specs=(
            P(None, "gx", "gy", None),
            P("gx", "gy", None),
            P(("gx", "gy"), None, None),
            P(),
            P(),
            P(("gx", "gy")),
            P(None, ("gx", "gy")),
        ),
        out_specs=(P(None, "gx", "gy", None), P(None, "gx", "gy", None)),
        check_vma=False,
    )
```

```python
import jax
import jax.numpy as jnp
from jax import lax
from jax.experimental import pallas as pl
from jax.experimental.pallas import tpu as pltpu
from jax.sharding import PartitionSpec as P

LAPLACE_COEFFS = (
    -5369.0 / 1800.0,
    12.0 / 7.0,
    -15.0 / 56.0,
    10.0 / 189.0,
    -1.0 / 112.0,
    2.0 / 1925.0,
    -1.0 / 16632.0,
)
SPACING = 0.4
CENTER = 45.0
HALF_WIDTH = 48.0
KINETIC = -0.5 / (SPACING * SPACING)
REACH = 6

ORB = 2
NPROJ = 9
LANES = 128
CX, CY, NZ = 32, 16, 256
SLOTS = 32
GROUPS = SLOTS // 8
ATOMS = 5120
WIDTH = 24
ATOM_LANE = 96
BLOCK = 8
COLUMN = 5 * BLOCK
PLANES = ORB * CX * 2
Y_ROWS = BLOCK + REACH * PLANES + 8
X_ROWS = ORB * REACH * 2 * CY

VMEM = pl.BlockSpec(memory_space=pltpu.VMEM)
SMEM = pl.BlockSpec(memory_space=pltpu.SMEM)
ANY = pl.BlockSpec(memory_space=pl.ANY)
HBM = pl.BlockSpec(memory_space=pltpu.HBM)
F32 = jnp.float32


def iota(shape, axis):
    return lax.broadcasted_iota(jnp.int32, shape, axis)


def swap_list_row(tiles):
    row = iota((8, LANES), 0)
    for d in (1, 2, 4):
        first = (row & d) == 0
        new = list(tiles)
        for k in range(8):
            if k & d == 0:
                low, high = (tiles[k], tiles[k | d])
                new[k] = jnp.where(first, low, pltpu.roll(high, d, 0))
                new[k | d] = jnp.where(first, pltpu.roll(low, 8 - d, 0), high)
        tiles = new
    return tiles


def turned(tile, lanes):
    return pltpu.roll(tile, lanes % LANES, 1) if lanes % LANES else tile


def swap_list_group(tiles):
    group = iota((8, LANES), 1) // 16
    tiles = [turned(tile, 16 * k) for k, tile in enumerate(tiles)]
    tiles = [tiles[-k % 8] for k in range(8)]
    for d in (1, 2, 4):
        moved = (group & d) != 0
        tiles = [jnp.where(moved, tiles[(k - d) % 8], tiles[k]) for k in range(8)]
    return [turned(tile, -16 * k) for k, tile in enumerate(tiles)]


def swap_groups(x):
    tiles = swap_list_row([x[k] for k in range(8)])
    return jnp.stack(swap_list_row(swap_list_group(tiles)))


def corner(offset_ref, slot):
    z = offset_ref[2, slot]
    return offset_ref[0, slot], offset_ref[1, slot], z // LANES, z % LANES


def rotate(work, rotated):
    for o in range(ORB):
        for x in range(CX):
            for half in range(2):
                for t in range(2):
                    rows = slice(8 * t, 8 * t + 8)
                    rotated[o, x, half, rows, :] = turned(work[o, x, half, rows, :], 16 * (x % 8))


def project(rotated, proj_ref, offset_ref, atom_ref, part):
    flat_lane = iota((BLOCK, LANES), 1)
    flat_row = iota((BLOCK, LANES), 0)
    block = jnp.zeros((BLOCK, LANES), F32)
    for s in range(SLOTS):
        place = (flat_row == s // 8) & (flat_lane == ATOM_LANE + s % 8)
        block = jnp.where(place, atom_ref[s].astype(F32), block)

    for g in range(GROUPS):
        slots = [[None] * 8 for _ in range(ORB)]
        for i in range(8):
            x, y, half, z = corner(offset_ref, g * 8 + i)
            place = flat_lane + (LANES - z)
            window = (place // 16 - x) & 7
            near = place % 16 < LANES - z
            shift = (4 * LANES + LANES - z - 16 * x) % LANES
            for o in range(ORB):
                low = rotated[o, x, half, pl.ds(y, 8), :]
                high = rotated[o, x, 1, pl.ds(y, 8), :]
                for a in range(1, 8):
                    here = window == a
                    low = jnp.where(here, rotated[o, x + a, half, pl.ds(y, 8), :], low)
                    high = jnp.where(here, rotated[o, x + a, 1, pl.ds(y, 8), :], high)
                slots[o][i] = pltpu.roll(jnp.where(near, low, high), shift, 1)
        patches = [swap_list_group(swap_list_row(tiles)) for tiles in slots]
        tile = jnp.zeros((8, LANES), F32)
        rows = slice(8 * g, 8 * g + 8)
        for p in range(NPROJ):
            values = [proj_ref[p, rows, LANES * a : LANES * (a + 1)] for a in range(8)]
            for o in range(ORB):
                total = values[0] * patches[o][0]
                for a in range(1, 8):
                    total = total + values[a] * patches[o][a]
                summed = jnp.sum(total, axis=1, keepdims=True)
                tile = jnp.where(flat_lane == 2 * p + o, summed, tile)
        block = block + turned(tile, g * WIDTH)

    part[...] = block


def pack_y(work, part, up, down):
    for n in range(PLANES):
        o, x, half = (n // (2 * CX), n // 2 % CX, n % 2)
        down[BLOCK + REACH * n : BLOCK + REACH * n + 8, :] = work[o, x, half, 0:8, :]
    for n in reversed(range(PLANES)):
        o, x, half = (n // (2 * CX), n // 2 % CX, n % 2)
        up[REACH * (n + 1) : REACH * (n + 1) + 8, :] = work[o, x, half, 8:16, :]
    for target in (up, down):
        if part is not None:
            target[0:BLOCK, :] = part[...]
        target[Y_ROWS - 8 : Y_ROWS, :] = jnp.zeros((8, LANES), F32)


def pack_x(work, x_up, x_down):
    for o in range(ORB):
        rows = slice(o * REACH * 32, (o + 1) * REACH * 32)
        x_up[rows, :] = work[o, CX - REACH : CX].reshape(REACH * 32, LANES)
        x_down[rows, :] = work[o, 0:REACH].reshape(REACH * 32, LANES)


def is_odd():
    return lax.axis_index("gy") % 2


def first_kernel(v, proj_hbm, offset_hbm, atom_hbm, y_pair, y_next, x_up, x_down, part,
                 work, rotated, proj_ref, offset_ref, atom_ref, block, packed, xs_up, xs_down,
                 sems):
    copies = [
        pltpu.make_async_copy(v.at[:, :, :, 0:LANES], work.at[:, :, 0], sems.at[0]),
        pltpu.make_async_copy(v.at[:, :, :, LANES:NZ], work.at[:, :, 1], sems.at[1]),
        pltpu.make_async_copy(offset_hbm, offset_ref, sems.at[2]),
        pltpu.make_async_copy(atom_hbm, atom_ref, sems.at[3]),
        pltpu.make_async_copy(proj_hbm, proj_ref, sems.at[4]),
    ]
    for copy in copies:
        copy.start()
    for copy in copies[:2]:
        copy.wait()
    pack_y(work, None, packed.at[0], packed.at[1])
    pack_x(work, xs_up, xs_down)
    odd = is_odd()
    halos = [
        pltpu.make_async_copy(
            source.at[pl.ds(start, rows)], target.at[pl.ds(start, rows)], sems.at[5 + k]
        )
        for k, (source, target, start, rows) in enumerate(
            (
                (packed.at[odd], y_pair, BLOCK, Y_ROWS - BLOCK),
                (packed.at[1 - odd], y_next, BLOCK, Y_ROWS - BLOCK),
                (xs_up, x_up, 0, X_ROWS),
                (xs_down, x_down, 0, X_ROWS),
            )
        )
    ]
    for copy in halos:
        copy.start()
    rotate(work, rotated)
    for copy in copies[2:]:
        copy.wait()
    project(rotated, proj_ref, offset_ref, atom_ref, block)
    blocks = [
        pltpu.make_async_copy(block, target.at[pl.ds(0, BLOCK)], sems.at[9 + k])
        for k, target in enumerate((y_pair, y_next, part))
    ]
    for copy in blocks:
        copy.start()
    for copy in halos + blocks:
        copy.wait()


def halves_of(field, split):
    if split:
        return [field[:, :, half] for half in range(2)]
    return [field[:, :, :, LANES * half : LANES * (half + 1)] for half in range(2)]


def local_kernel(scale, second, *refs):
    if second:
        field, potential, orbital, out, pad = refs
    else:
        field, potential, out, pad = refs
    halves = halves_of(field, second)
    weights = [scale * KINETIC / HALF_WIDTH * w for w in LAPLACE_COEFFS]
    for o in range(ORB):
        for x in range(REACH):
            pad[o, x, :, 8:24, :] = jnp.zeros((2, CY, LANES), F32)
            pad[o, x + REACH + CX, :, 8:24, :] = jnp.zeros((2, CY, LANES), F32)
        pad[o, REACH : REACH + CX, :, 0:8, :] = jnp.zeros((CX, 2, 8, LANES), F32)
        pad[o, REACH : REACH + CX, :, 24:32, :] = jnp.zeros((CX, 2, 8, LANES), F32)
        for half in range(2):
            pad[o, REACH : REACH + CX, half, 8:24, :] = halves[half][o]

    def step(n, carry):
        o, x = (n // (CX // 4), n % (CX // 4) * 4)
        for half in range(2):
            lanes = slice(LANES * half, LANES * (half + 1))
            for t in range(2):
                rows = slice(8 + 8 * t, 16 + 8 * t)
                line = [pad[o, x + k, half, rows, :] for k in range(4 + 2 * REACH)]
                for q in range(4):
                    factor = potential[x + q, 8 * t : 8 * t + 8, lanes] * (scale / HALF_WIDTH) + (
                        3.0 * weights[0] - scale * CENTER / HALF_WIDTH
                    )
                    middle = q + REACH
                    total = factor * line[middle]
                    for r in range(1, REACH + 1):
                        paired = line[middle + r] + line[middle - r]
                        paired = paired + (
                            pad[o, x + middle, half, 8 + 8 * t + r : 16 + 8 * t + r, :]
                            + pad[o, x + middle, half, 8 + 8 * t - r : 16 + 8 * t - r, :]
                        )
                        total = total + weights[r] * paired
                    if second:
                        total = total - orbital[o, x + q, 8 * t : 8 * t + 8, lanes]
                    out[o, x + q, half, 8 * t : 8 * t + 8, :] = total
        return carry

    lax.fori_loop(0, ORB * CX // 4, step, 0)


def edge_kernel(scale, second, pair_ref, next_ref, local, field, *refs):
    if second:
        full, out, along_z, before, after, sems = refs
    else:
        out, along_z, before, after, sems = refs
    odd = is_odd()
    even_copies = [
        pltpu.make_async_copy(next_ref, before, sems.at[0]),
        pltpu.make_async_copy(pair_ref, after, sems.at[1]),
    ]
    odd_copies = [
        pltpu.make_async_copy(pair_ref, before, sems.at[0]),
        pltpu.make_async_copy(next_ref, after, sems.at[1]),
    ]

    @pl.when(odd == 0)
    def _():
        for copy in even_copies:
            copy.start()

    @pl.when(odd == 1)
    def _():
        for copy in odd_copies:
            copy.start()

    halves = halves_of(field, second)
    if second:
        fulls = [
            pltpu.make_async_copy(
                field.at[:, :, half],
                full.at[:, :, :, LANES * half : LANES * (half + 1)],
                sems.at[2 + half],
            )
            for half in range(2)
        ]
        for copy in fulls:
            copy.start()
    gap = jnp.abs(iota((NZ, NZ), 0) - iota((NZ, NZ), 1))
    band = jnp.zeros((NZ, NZ), F32)
    for r in range(1, REACH + 1):
        weight = scale * KINETIC / HALF_WIDTH * LAPLACE_COEFFS[r]
        band = jnp.where(gap == r, weight, band)
    values = jnp.concatenate(
        [half.reshape(ORB * CX * CY, LANES) for half in halves], axis=1
    )
    value_high = values.astype(jnp.bfloat16)
    value_low = (values - value_high.astype(F32)).astype(jnp.bfloat16)
    band_high = band.astype(jnp.bfloat16)
    band_low = (band - band_high.astype(F32)).astype(jnp.bfloat16)
    summed = jnp.dot(value_high, band_high, preferred_element_type=F32)
    summed = summed + jnp.dot(value_low, band_high, preferred_element_type=F32)
    summed = summed + jnp.dot(value_high, band_low, preferred_element_type=F32)
    along_z[...] = summed
    row = iota((8, LANES), 0)
    low, high = ([None], [None])
    for r in range(1, REACH + 1):
        weight = scale * KINETIC / HALF_WIDTH * LAPLACE_COEFFS[r]
        low.append(jnp.where(row < r, weight, 0.0).astype(F32))
        high.append(jnp.where(row >= 8 - r, weight, 0.0).astype(F32))

    @pl.when(odd == 0)
    def _():
        for copy in even_copies:
            copy.wait()

    @pl.when(odd == 1)
    def _():
        for copy in odd_copies:
            copy.wait()

    def step(n, carry):
        o, x = (n // CX, n % CX)
        depth = pl.multiple_of(n * CY, CY)
        for half in range(2):
            lanes = slice(LANES * half, LANES * (half + 1))
            start = (n * 2 + half) * REACH
            first = local[o, x, half, 0:8, :] + along_z[pl.ds(depth, 8), lanes]
            second_rows = local[o, x, half, 8:16, :] + along_z[pl.ds(depth + 8, 8), lanes]
            for r in range(1, REACH + 1):
                first = first + low[r] * before[pl.ds(start + BLOCK + REACH - r, 8), :]
                second_rows = second_rows + high[r] * after[pl.ds(start + r, 8), :]
            out[o, x, half, 0:8, :] = first
            out[o, x, half, 8:16, :] = second_rows
        return carry

    lax.fori_loop(0, ORB * CX, step, 0, unroll=4)
    if second:
        for copy in fulls:
            copy.wait()


def gather_kernel(pair, after_pair, part, chips, after_chips, x_up_in, x_down_in, local,
                  x_up, x_down, column, sems):
    sources = (
        pair.at[0:BLOCK],
        after_pair.at[0:BLOCK],
        part,
        chips,
        after_chips,
    )
    copies = []
    for k, source in enumerate(sources):
        for n, (target, start) in enumerate(((x_up, X_ROWS), (x_down, X_ROWS), (column, 0))):
            rows = pl.ds(start + BLOCK * k, BLOCK)
            copies.append(pltpu.make_async_copy(source, target.at[rows], sems.at[3 * k + n]))
    for copy in copies:
        copy.start()
    for copy in copies:
        copy.wait()


def coefficients(columns, atom_ref):
    row = iota((8, LANES), 0)
    lane = iota((BLOCK, LANES), 1)
    own = []
    for g in range(GROUPS):
        held = jnp.full((8, LANES), -1.0, F32)
        for i in range(8):
            atom = atom_ref[8 * g + i]
            atom = jnp.where(atom < ATOMS, atom, -1)
            held = jnp.where(row == i, atom.astype(F32), held)
        own.append(held)
    own = jnp.concatenate(own, axis=0)
    result = jnp.zeros((GROUPS * SLOTS, 3 * LANES), F32)
    for values in columns:
        high = values.astype(jnp.bfloat16)
        rest = values - high.astype(F32)
        middle = rest.astype(jnp.bfloat16)
        low = (rest - middle.astype(F32)).astype(jnp.bfloat16)
        atoms = jnp.full((BLOCK, LANES), -2.0, F32)
        for k in range(5):
            tile = values[BLOCK * k : BLOCK * (k + 1)]
            moved = pltpu.roll(tile, LANES - ATOM_LANE + 8 * k, 1)
            atoms = jnp.where(lane // 8 == k, moved, atoms)
        same = jnp.concatenate(
            [jnp.where(own == atoms[g : g + 1, :], 1.0, 0.0) for g in range(GROUPS)], axis=0
        )
        same = same[:, :COLUMN].astype(jnp.bfloat16)
        result = result + jnp.dot(
            same, jnp.concatenate([high, middle, low], axis=1), preferred_element_type=F32
        )
    result = result[:, :LANES] + result[:, LANES : 2 * LANES] + result[:, 2 * LANES :]
    total = result[:SLOTS]
    for g in range(1, GROUPS):
        total = total + pltpu.roll(result[SLOTS * g : SLOTS * (g + 1)], LANES - WIDTH * g, 1)
    return total


def finish(scale, local, before, after, two_before, two_after, column, proj_ref,
           strength_ref, offset_ref, atom_ref, work, table, held, split, extra):
    weights = [scale * KINETIC / HALF_WIDTH * w for w in LAPLACE_COEFFS]
    extra[...] = jnp.zeros(WORK, F32)
    count = 0
    for s in range(SLOTS):
        split[count] = s
        z = offset_ref[2, s]
        count = count + jnp.where((z > LANES - 16) & (z < LANES), 1, 0)
    table[...] = coefficients(
        (
            column[...],
            before[X_ROWS:, :],
            after[X_ROWS:, :],
            two_before[...],
            two_after[...],
        ),
        atom_ref,
    )
    for o in range(ORB):
        for j in range(REACH):
            low = local[o, j]
            for i in range(j, REACH):
                rows = slice((o * REACH + i) * 32, (o * REACH + i + 1) * 32)
                low = low + weights[j + REACH - i] * before[rows, :].reshape(2, CY, LANES)
            work[o, j] = low
            high = local[o, CX - REACH + j]
            for i in range(j + 1):
                rows = slice((o * REACH + i) * 32, (o * REACH + i + 1) * 32)
                high = high + weights[REACH + i - j] * after[rows, :].reshape(2, CY, LANES)
            work[o, CX - REACH + j] = high

    lane = iota((8, LANES), 1)

    def windows(slot):
        x, y, half, z = corner(offset_ref, slot)
        place = lane + (LANES - z)
        return x, y, half, z, (place // 16 - x) & 7, place % 16 < LANES - z

    for g in range(GROUPS):
        rows = slice(8 * g, 8 * g + 8)
        factors = table[rows, :]
        added = [[None] * 8 for _ in range(ORB)]
        for p in range(NPROJ):
            strength = strength_ref[p] * (scale / HALF_WIDTH)
            spread = [
                jnp.broadcast_to(factors[:, 2 * p + o : 2 * p + o + 1], (8, LANES)) * strength
                for o in range(ORB)
            ]
            for a in range(8):
                values = proj_ref[p, rows, LANES * a : LANES * (a + 1)]
                for o in range(ORB):
                    term = values * spread[o]
                    added[o][a] = term if p == 0 else added[o][a] + term
        slots = [swap_list_row(swap_list_group(added[o])) for o in range(ORB)]
        for i in range(8):
            x, y, half, z, window, near = windows(g * 8 + i)
            shift = (z + 16 * x) % LANES
            moved = [pltpu.roll(slots[o][i], shift, 1) for o in range(ORB)]
            for o in range(ORB):
                held[g, o, i] = moved[o]
            sums = []
            for a in range(8):
                here = (window == a) & near
                for o in range(ORB):
                    sums.append(
                        extra[o, x + a, half, pl.ds(y, 8), :] + jnp.where(here, moved[o], 0.0)
                    )
            for a in range(8):
                for o in range(ORB):
                    extra[o, x + a, half, pl.ds(y, 8), :] = sums[ORB * a + o]

    def split_step(n, carry):
        s = split[n]
        x, y, half, z, window, near = windows(s)
        for a in range(8):
            here = (window == a) & jnp.logical_not(near)
            for o in range(ORB):
                place = (o, x + a, 1, pl.ds(y, 8), slice(None))
                extra[place] = extra[place] + jnp.where(here, held[s // 8, o, s % 8], 0.0)
        return carry

    lax.fori_loop(0, count, split_step, 0)
    for o in range(ORB):
        for x in range(CX):
            base = local if REACH <= x < CX - REACH else work
            for half in range(2):
                for t in range(2):
                    place = (o, x, half, slice(8 * t, 8 * t + 8), slice(None))
                    work[place] = base[place] + turned(extra[place], -16 * (x % 8))


def middle_kernel(scale, local, before_ref, after_ref, two_before, two_after, column, proj_ref,
                  strength_ref, offset_ref, atom_ref, work, y_pair, y_next, x_up, x_down, part,
                  rotated, *scratch):
    finish(scale, local, before_ref, after_ref, two_before, two_after, column, proj_ref,
           strength_ref, offset_ref, atom_ref, work, *scratch)
    rotate(work, rotated)
    project(rotated, proj_ref, offset_ref, atom_ref, part)
    pack_x(work, x_up, x_down)
    odd = is_odd()

    @pl.when(odd == 0)
    def _():
        pack_y(work, part, y_pair, y_next)

    @pl.when(odd == 1)
    def _():
        pack_y(work, part, y_next, y_pair)


def last_kernel(scale, local, before_ref, after_ref, two_before, two_after, column, proj_ref,
                strength_ref, offset_ref, atom_ref, out, work, *scratch):
    *scratch, sems = scratch
    finish(scale, local, before_ref, after_ref, two_before, two_after, column, proj_ref,
           strength_ref, offset_ref, atom_ref, work, *scratch)
    copies = [
        pltpu.make_async_copy(
            work.at[:, :, half], out.at[:, :, :, LANES * half : LANES * (half + 1)], sems.at[half]
        )
        for half in range(2)
    ]
    for copy in copies:
        copy.start()
    for copy in copies:
        copy.wait()


def shaped(*shape):
    return jax.ShapeDtypeStruct(shape, F32)


PARAMS = pltpu.CompilerParams(vmem_limit_bytes=16 * 1024 * 1024)
FIELD = (ORB, CX, CY, NZ)
WORK = (ORB, CX, 2, CY, LANES)
SENT = (
    shaped(Y_ROWS, LANES),
    shaped(Y_ROWS, LANES),
    shaped(X_ROWS + COLUMN, LANES),
    shaped(X_ROWS + COLUMN, LANES),
    shaped(BLOCK, LANES),
)


def cost(microseconds):
    return pl.CostEstimate(
        flops=0, transcendentals=0, bytes_accessed=int(microseconds * 3.0e6)
    )


def shift(value, axis, step):
    devices = lax.axis_size(axis)
    return lax.ppermute(value, axis, [(i, (i + step) % devices) for i in range(devices)])


def swapped(value, span, later):
    devices = lax.axis_size("gy")
    pairs = []
    for i in range(devices):
        up = (i // span + later) % 2 == 0
        pairs.append((i, (i + (span if up else -span)) % devices))
    return lax.ppermute(value, "gy", pairs)


def local_part(scale, field, potential, orbital):
    second = orbital is not None
    args = (field, potential) + ((orbital,) if second else ())

    def local_body(*refs):
        local_kernel(scale, second, *refs)

    return pl.pallas_call(
        local_body,
        out_shape=shaped(*WORK),
        in_specs=[VMEM] * len(args),
        out_specs=VMEM,
        scratch_shapes=[pltpu.VMEM((ORB, CX + 2 * REACH, 2, 32, LANES), F32)],
        compiler_params=PARAMS,
        cost_estimate=cost(4),
        name="local_part",
    )(*args)


def edge_part(scale, before, after, local, field, second):
    def edge_body(*refs):
        edge_kernel(scale, second, *refs)

    return pl.pallas_call(
        edge_body,
        out_shape=(shaped(*FIELD), shaped(*WORK)) if second else shaped(*WORK),
        in_specs=[ANY, ANY, VMEM, VMEM],
        out_specs=(HBM, VMEM) if second else VMEM,
        scratch_shapes=[pltpu.VMEM((ORB * CX * CY, NZ), F32)]
        + [pltpu.VMEM((Y_ROWS, LANES), F32)] * 2
        + [pltpu.SemaphoreType.DMA((4,))],
        compiler_params=PARAMS,
        cost_estimate=cost(2),
        name="edge_part",
    )(before, after, local, field)


def gather_part(pair, after_pair, part, chips, after_chips, x_up, x_down, local):
    return pl.pallas_call(
        gather_kernel,
        out_shape=(SENT[2], SENT[3], shaped(COLUMN, LANES)),
        in_specs=[ANY] * 8,
        out_specs=(ANY,) * 3,
        scratch_shapes=[pltpu.SemaphoreType.DMA((15,))],
        input_output_aliases={5: 0, 6: 1},
        compiler_params=PARAMS,
        cost_estimate=cost(1),
        name="gather_part",
    )(pair, after_pair, part, chips, after_chips, x_up, x_down, local)


def apply(scale, field, potential, sent, orbital, shared):
    second = orbital is not None
    y_pair, y_next, x_up, x_down, part = sent
    projectors, strengths, offsets, atoms = shared
    next_one = swapped(y_next, 1, 1)
    next_two = swapped(part, 2, 1)
    pair_two = swapped(part, 2, 0)
    pair_one = swapped(y_pair, 1, 0)
    if not second:
        field, part = lax.optimization_barrier((field, part))
    local = local_part(scale, field, potential, orbital)
    x_up, x_down, column = gather_part(
        pair_one, next_one, part, pair_two, next_two, x_up, x_down, local
    )
    x_before = shift(x_up, "gx", 1)
    x_after = shift(x_down, "gx", -1)
    x_two_before = shift(column, "gx", 2)
    x_two_after = shift(column, "gx", -2)
    local = edge_part(scale, pair_one, next_one, local, field, second)
    if second:
        full, local = local
    kernel = last_kernel if second else middle_kernel

    def end_body(*refs):
        kernel(scale, *refs)

    scratch = [
        pltpu.VMEM((SLOTS, LANES), F32),
        pltpu.VMEM((GROUPS, ORB, 8, 8, LANES), F32),
        pltpu.SMEM((SLOTS + 1,), jnp.int32),
        pltpu.VMEM(WORK, F32),
    ]
    result = pl.pallas_call(
        end_body,
        out_shape=shaped(*FIELD) if second else (shaped(*WORK),) + SENT,
        in_specs=[VMEM] * 7 + [SMEM] * 3,
        out_specs=HBM if second else (VMEM,) * 6,
        scratch_shapes=[pltpu.VMEM(WORK, F32)]
        + scratch
        + ([pltpu.SemaphoreType.DMA((2,))] if second else []),
        compiler_params=PARAMS,
        cost_estimate=cost(6),
        name="last_part" if second else "middle_part",
    )(local, x_before, x_after, x_two_before, x_two_after, column, projectors, strengths, offsets,
      atoms)
    return (full, result) if second else result


def shards(orbitals, potential, projectors, strengths, atom_owner, slot_atom, slot_offset):
    projectors = jnp.transpose(projectors, (1, 0, 2))
    shared = (projectors, strengths, slot_offset, slot_atom)
    sent = pl.pallas_call(
        first_kernel,
        out_shape=SENT,
        in_specs=[HBM] * 4,
        out_specs=(HBM,) * 5,
        scratch_shapes=[
            pltpu.VMEM(WORK, F32),
            pltpu.VMEM(WORK, F32),
            pltpu.VMEM((NPROJ, SLOTS, 8 * LANES), F32),
            pltpu.SMEM((3, SLOTS), jnp.int32),
            pltpu.SMEM((SLOTS,), jnp.int32),
            pltpu.VMEM((BLOCK, LANES), F32),
            pltpu.VMEM((2, Y_ROWS, LANES), F32),
            pltpu.VMEM((X_ROWS, LANES), F32),
            pltpu.VMEM((X_ROWS, LANES), F32),
            pltpu.SemaphoreType.DMA((12,)),
        ],
        compiler_params=pltpu.CompilerParams(vmem_limit_bytes=60 * 1024 * 1024),
        cost_estimate=cost(3),
        name="first_part",
    )(orbitals, projectors, slot_offset, slot_atom)
    field, *sent = apply(1.0, orbitals, potential, sent, None, shared)
    return apply(2.0, field, potential, sent, orbitals, shared)


def solution(mesh):
    return jax.shard_map(
        shards,
        mesh=mesh,
        in_specs=(
            P(None, "gx", "gy", None),
            P("gx", "gy", None),
            P(("gx", "gy"), None, None),
            P(),
            P(),
            P(("gx", "gy")),
            P(None, ("gx", "gy")),
        ),
        out_specs=(P(None, "gx", "gy", None), P(None, "gx", "gy", None)),
        check_vma=False,
    )
```
